128 devices in a mesh: ray: 4 (over y), mp: 32 (over x, z, core).
Axes of the slice: x: 4, y: 4, z: 4, core: 2. Of those that a mesh axis runs over, the one named last changes fastest.
Arguments:
- coeffs_start: float32 [131072, 128], P('mp', 'ray'), may hold values from -6 to 6
- observed: float32 [32768, 128], P('ray'), may hold values from -6 to 6
- jacobian_tiles: bfloat16 [4, 32, 384, 128, 128], P('ray', 'mp'), may hold values from -0.0625 to 0.0625
- tile_rows: int32 [4, 32, 384], P('ray', 'mp'), may hold values from 0 to 63, as said below
- tile_cols: int32 [4, 32, 384], P('ray', 'mp'), may hold values from 0 to 31, as said below
- tile_count: int32 [4, 32], P('ray', 'mp'), may hold values from 48 to 384, as said below
Outputs:
- coefficients: float32 [131072, 128], P('mp', 'ray')
- misfit: float32 [32768, 128], P(('ray', 'mp'))
The draws below stay inside these ranges and needn't reach their ends.
Inputs may be any that keep to these rules, and one draw needn't show every extreme that they name: `tile_count`: every device has at least 48 live slots, and one device has all 384. `tile_rows`: the 384 slots of one device name distinct pairs of ray block and cell tile. `tile_cols`: the 384 slots of one device name distinct pairs of ray block and cell tile.
All inputs are finite; a program needn't handle non-finite values.
Results may differ from the reference program's by a relative error of at most 0.0053.
Values may be sent and summed in bfloat16 or wider, within the bound.
No kernel may reach another device: no remote copies, remote signals or barrier semaphores. Data moves between devices by JAX's collectives and lax.ppermute only.
A program may use at most 128 MiB of HBM per device.

```python
import math
import jax
import jax.numpy as jnp
from jax import lax

TILE = 128
CTD = 32
RBD = 64
TPD = 384
MEMBERS = 128
LEVELS = 5
ITERS = 2
CELLS_DEV = 4096
RAY_GROUPS = 4
MODEL_GROUPS = 32
CELLS = 131072
RAYS = 32768


def tile_pattern(key):
    base = jax.random.fold_in(key, 11)
    device_keys = jax.random.split(base, RAY_GROUPS * MODEL_GROUPS)

    def one_device(device_key):
        return jax.random.permutation(device_key, RBD * CTD)[:TPD]
    flat = jax.vmap(one_device)(device_keys).astype(jnp.int32)
    return flat.reshape(RAY_GROUPS, MODEL_GROUPS, TPD)


def draw_tile_rows(key, part):
    return (tile_pattern(key) // CTD).astype(jnp.int32)


def draw_tile_cols(key, part):
    return (tile_pattern(key) % CTD).astype(jnp.int32)


def draw_tile_count(key, part):
    base = jax.random.fold_in(key, 23)
    first_key, second_key = jax.random.split(base)
    counts = jax.random.randint(first_key, (RAY_GROUPS * MODEL_GROUPS,), TPD // 8, TPD // 2 + 1)
    busiest = jax.random.randint(second_key, (), 0, RAY_GROUPS * MODEL_GROUPS)
    counts = jnp.where(jnp.arange(RAY_GROUPS * MODEL_GROUPS) == busiest, TPD, counts)
    return counts.reshape(RAY_GROUPS, MODEL_GROUPS).astype(jnp.int32)


def level_of(key, dims, cuts, low, high):
    def one(position, shards_of):
        steps = jax.random.uniform(jax.random.fold_in(jax.random.fold_in(key, 6), position), (shards_of,), jnp.float32, low / len(cuts), high / len(cuts))
        return jnp.repeat(jnp.exp(steps), dims[position] // shards_of).reshape((-1,) + (1,) * (len(dims) - position - 1))

    level = one(*cuts[0])
    for cut in cuts[1:]:
        level = level * one(*cut)
    return level


def normal_values(own_key, shape, width, limit, shards=(), kind=jnp.bfloat16):
    entries = jax.random.normal(own_key, shape, jnp.float32) * width
    if len(shards) > 0:
        entries = level_of(own_key, shape, shards, -0.22, 0.18) * entries
    return jnp.clip(entries, min=-limit, max=limit).astype(kind)


def setup_inputs(seed: int = 0) -> dict:
    keys = jax.random.split(jax.random.key(seed), 7)
    return {
        "coeffs_start": normal_values(keys[0], (CELLS, MEMBERS), 1.0, 6.0, ((0, 32), (1, 4)), jnp.float32),
        "observed": normal_values(keys[1], (RAYS, MEMBERS), 1.0, 6.0, ((0, 4),), jnp.float32),
        "jacobian_tiles": normal_values(keys[2], (RAY_GROUPS, MODEL_GROUPS, TPD, TILE, TILE), (TILE * TPD * MODEL_GROUPS // (3 * RBD)) ** -0.5, 0.0625, ((0, 4), (1, 32))),
        "tile_rows": draw_tile_rows(jax.random.fold_in(keys[6], 71), 0),
        "tile_cols": draw_tile_cols(jax.random.fold_in(keys[6], 71), 0),
        "tile_count": draw_tile_count(jax.random.fold_in(keys[6], 71), 0),
    }


root_three = math.sqrt(3.0)
norm_factor = 4.0 * math.sqrt(2.0)
low_pass = [(1.0 + root_three) / norm_factor, (3.0 + root_three) / norm_factor, (3.0 - root_three) / norm_factor, (1.0 - root_three) / norm_factor]
high_pass = [low_pass[3], -low_pass[2], low_pass[1], -low_pass[0]]
step_length = 0.5
threshold = 0.1

def analyse_level(signal):
    even_part = signal[0::2]
    odd_part = signal[1::2]
    even_next = jnp.roll(even_part, -1, axis=0)
    odd_next = jnp.roll(odd_part, -1, axis=0)
    smooth = low_pass[0] * even_part + low_pass[1] * odd_part + low_pass[2] * even_next + low_pass[3] * odd_next
    detail = high_pass[0] * even_part + high_pass[1] * odd_part + high_pass[2] * even_next + high_pass[3] * odd_next
    return (smooth, detail)

def synthesise_level(smooth, detail):
    smooth_prev = jnp.roll(smooth, 1, axis=0)
    detail_prev = jnp.roll(detail, 1, axis=0)
    even_part = low_pass[0] * smooth + high_pass[0] * detail + low_pass[2] * smooth_prev + high_pass[2] * detail_prev
    odd_part = low_pass[1] * smooth + high_pass[1] * detail + low_pass[3] * smooth_prev + high_pass[3] * detail_prev
    return jnp.stack([even_part, odd_part], axis=1).reshape((-1, smooth.shape[1]))

def analyse(cells):
    members_here = cells.shape[1]
    signal = cells
    blocks = []
    for level_index in range(LEVELS):
        signal, detail = analyse_level(signal)
        blocks.append(detail.reshape(MODEL_GROUPS, -1, members_here))
    blocks.append(signal.reshape(MODEL_GROUPS, -1, members_here))
    return jnp.concatenate(blocks, axis=1).reshape(-1, members_here)

def synthesise(coeffs):
    members_here = coeffs.shape[1]
    blocks = coeffs.reshape(MODEL_GROUPS, CELLS_DEV, members_here)
    details = []
    offset = 0
    for level_index in range(LEVELS):
        length = CELLS_DEV >> level_index + 1
        details.append(blocks[:, offset:offset + length].reshape(-1, members_here))
        offset = offset + length
    signal = blocks[:, offset:].reshape(-1, members_here)
    for level_index in reversed(range(LEVELS)):
        signal = synthesise_level(signal, details[level_index])
    return signal

def shrink_update(coeffs, gradient):
    moved = coeffs - step_length * gradient
    shrunk = moved - jnp.clip(moved, -threshold, threshold)
    local_rows = jnp.arange(CELLS_DEV)
    is_smooth = jnp.tile(local_rows >= CELLS_DEV - (CELLS_DEV >> LEVELS), MODEL_GROUPS)[:, None]
    return jnp.where(is_smooth, moved, shrunk)

def forward_all(jacobian_tiles, tile_rows, tile_cols, tile_count, model_cells):
    members_here = model_cells.shape[1]
    cell_blocks = model_cells.reshape(MODEL_GROUPS, CTD, TILE, members_here)
    slot_index = jnp.arange(TPD)

    def one_device(running, device_flat):
        ray_group = device_flat // MODEL_GROUPS
        model_group = device_flat % MODEL_GROUPS
        tile_values = jacobian_tiles[ray_group, model_group].astype(jnp.float32)
        live = (slot_index < tile_count[ray_group, model_group]).astype(jnp.float32)
        picked = cell_blocks[model_group][tile_cols[ray_group, model_group]].astype(jnp.float32)
        products = jnp.einsum('sij,sjb->sib', tile_values, picked) * live[:, None, None]
        partial_rows = jax.ops.segment_sum(products, tile_rows[ray_group, model_group], num_segments=RBD)
        return (running.at[ray_group].add(partial_rows), None)
    start_value = jnp.zeros((RAY_GROUPS, RBD, TILE, members_here), jnp.float32)
    running, unused = lax.scan(one_device, start_value, jnp.arange(RAY_GROUPS * MODEL_GROUPS))
    return running.reshape(-1, members_here)

def backward_all(jacobian_tiles, tile_rows, tile_cols, tile_count, misfit_rounded):
    members_here = misfit_rounded.shape[1]
    ray_blocks = misfit_rounded.reshape(RAY_GROUPS, RBD, TILE, members_here)
    slot_index = jnp.arange(TPD)

    def one_device(running, device_flat):
        ray_group = device_flat // MODEL_GROUPS
        model_group = device_flat % MODEL_GROUPS
        tile_values = jacobian_tiles[ray_group, model_group].astype(jnp.float32)
        live = (slot_index < tile_count[ray_group, model_group]).astype(jnp.float32)
        picked = ray_blocks[ray_group][tile_rows[ray_group, model_group]].astype(jnp.float32)
        products = jnp.einsum('sij,sib->sjb', tile_values, picked) * live[:, None, None]
        partial_cells = jax.ops.segment_sum(products, tile_cols[ray_group, model_group], num_segments=CTD)
        return (running.at[model_group].add(partial_cells), None)
    start_value = jnp.zeros((MODEL_GROUPS, CTD, TILE, members_here), jnp.float32)
    running, unused = lax.scan(one_device, start_value, jnp.arange(RAY_GROUPS * MODEL_GROUPS))
    return running.reshape(-1, members_here)

def reference(coeffs_start, observed, jacobian_tiles, tile_rows, tile_cols, tile_count):
    coeffs = coeffs_start
    misfit = observed
    for sweep_index in range(ITERS):
        model_cells = synthesise(coeffs).astype(jnp.bfloat16)
        misfit = forward_all(jacobian_tiles, tile_rows, tile_cols, tile_count, model_cells) - observed
        back_terms = backward_all(jacobian_tiles, tile_rows, tile_cols, tile_count, misfit.astype(jnp.bfloat16))
        coeffs = shrink_update(coeffs, analyse(back_terms))
    return (coeffs, misfit)
```

```python
import math

import jax
import jax.numpy as jnp
from jax import lax
from jax.experimental import pallas as pl
from jax.experimental.pallas import tpu as pltpu
from jax.sharding import Mesh, PartitionSpec as P

LEVELS = 5
ITERS = 2
TILE = 128
UNROLL = 8
CHUNK = 16

root_three = math.sqrt(3.0)
norm_factor = 4.0 * math.sqrt(2.0)
low_pass = [
    (1.0 + root_three) / norm_factor,
    (3.0 + root_three) / norm_factor,
    (3.0 - root_three) / norm_factor,
    (1.0 - root_three) / norm_factor,
]
high_pass = [low_pass[3], -low_pass[2], low_pass[1], -low_pass[0]]
step_length = 0.5
threshold = 0.1

f32 = jnp.float32
bf16 = jnp.bfloat16

SEG_ROWS = [512, 256, 128, 64, 32, 32]
SEG_OFF = [0]
for n in SEG_ROWS:
    SEG_OFF.append(SEG_OFF[-1] + 8 + n)
STATE_ROWS = SEG_OFF[-1]
COEF_OFF = [0, 2048, 3072, 3584, 3840, 3968]

VM = pl.BlockSpec(memory_space=pltpu.VMEM)
SM = pl.BlockSpec(memory_space=pltpu.SMEM)
ANY = pl.BlockSpec(memory_space=pl.ANY)


def sds(shape, dtype):
    return jax.ShapeDtypeStruct(shape, dtype)


def call(kernel, name, in_specs, outs, scratch=(), mib=40):
    return pl.pallas_call(
        kernel,
        name=name,
        in_specs=in_specs,
        out_specs=[VM] * len(outs),
        out_shape=outs,
        scratch_shapes=list(scratch),
        compiler_params=pltpu.CompilerParams(vmem_limit_bytes=mib * 1024 * 1024),
    )


def lanes(shape):
    return lax.broadcasted_iota(jnp.int32, shape, 1)


def init_kernel(coeffs, state, tails):
    for g in range(6):
        n = SEG_ROWS[g]
        base = SEG_OFF[g]
        parts = [coeffs[COEF_OFF[g] + q * n : COEF_OFF[g] + (q + 1) * n, :] for q in range(4)]
        packed = jnp.concatenate(parts, axis=1)
        state[base + 8 : base + 8 + n, :] = packed
        last = packed[n - 8 : n, :]
        state[base : base + 8, :] = pltpu.roll(last, 32, 1)
        tails[8 * g : 8 * g + 8, :] = last


def synth_from(state, bufs, model_t):
    src = None
    for level in reversed(range(LEVELS)):
        n = SEG_ROWS[level]
        base = SEG_OFF[level]
        if src is None:
            sm = state[SEG_OFF[5] + 4 : SEG_OFF[5] + 8 + n, :]
            sp = state[SEG_OFF[5] + 3 : SEG_OFF[5] + 7 + n, :]
        else:
            sm = src[4 : 8 + n, :]
            sp = src[3 : 7 + n, :]
        dm = state[base + 4 : base + 8 + n, :]
        dp = state[base + 3 : base + 7 + n, :]
        even = low_pass[0] * sm + high_pass[0] * dm + low_pass[2] * sp + high_pass[2] * dp
        odd = low_pass[1] * sm + high_pass[1] * dm + low_pass[3] * sp + high_pass[3] * dp
        dst = bufs[level]
        dst[pl.ds(0, n + 4, stride=2), :] = even
        dst[pl.ds(1, n + 4, stride=2), :] = odd
        src = dst
    for i in range(8):
        tile = src[8 + 128 * i : 8 + 128 * (i + 1), :]
        model_t[i] = tile.T.astype(bf16)


SYNTH_BUFS = [pltpu.VMEM((8 + 2 * SEG_ROWS[l], 128), f32) for l in range(LEVELS)]


def synth_kernel(state_in, recv, state, model_t, *bufs):
    state[...] = state_in[...]
    for g in range(6):
        base = SEG_OFF[g]
        own = state_in[base : base + 8, :]
        got = pltpu.roll(recv[8 * g : 8 * g + 8, :], 32, 1)
        state[base : base + 8, :] = jnp.where(lanes((8, 128)) < 32, got, own)
    synth_from(state, bufs, model_t)


def fwd_kernel(rows, cols, cnt, place, p0, p1, p2, p3, jac, keep, send, jbuf, model, acc, sems):
    live = cnt[0]
    core = place[2]
    n_chunks = (live + CHUNK - 1) // CHUNK
    total = jac.shape[0] // CHUNK

    def copy(i):
        return pltpu.make_async_copy(
            jac.at[pl.ds(i * CHUNK, CHUNK)], jbuf.at[pl.ds(i * CHUNK, CHUNK)], sems.at[i]
        )

    for i in range(total):
        @pl.when(i < n_chunks)
        def _():
            copy(i).start()

    acc[...] = jnp.zeros(acc.shape, f32)
    for c in range(32):
        q, t = c // 8, c % 8
        for k, piece in enumerate((p0, p1, p2, p3)):
            model[c, 32 * k : 32 * k + 32, :] = piece[t, 32 * q : 32 * q + 32, :]

    def chunk(i, carry):
        copy(i).wait()
        for u in range(CHUNK // UNROLL):
            for v in range(UNROLL):
                s = i * CHUNK + u * UNROLL + v
                r = jnp.where(s < live, rows[s], 64)
                prod = lax.dot_general(
                    model[cols[s]], jbuf[s], (((1,), (1,)), ((), ())), preferred_element_type=f32
                )
                acc[r] += prod
        return carry

    lax.fori_loop(0, n_chunks, chunk, 0)
    for xz in range(16):
        for h in range(2):
            keep[2 * xz + h] = acc[4 * xz + 2 * core + h]
            send[2 * xz + h] = acc[4 * xz + 2 * (1 - core) + h].astype(bf16)


def split_kernel(place, keep, recv, own, s1, s2, s3):
    x = place[0]
    for k, out in enumerate((own, s1, s2, s3)):
        b = 8 * ((x + k) % 4)
        for i in range(8):
            out[i] = (keep[b + i] + recv[b + i].astype(f32)).astype(out.dtype)


def gather_kernel(own, r1, r2, r3, total, sent):
    for i in range(8):
        s = own[i] + r1[i].astype(f32) + r2[i].astype(f32) + r3[i].astype(f32)
        total[i] = s
        sent[i] = s.astype(bf16)


def obs_kernel(place, obs, out, buf):
    r = place[3]
    for i in range(8):
        buf[...] = obs[i // 2, 128 * (i % 2) : 128 * (i % 2) + 128, :].T
        for k in range(4):
            out[i, 32 * k : 32 * k + 32, :] = buf[pl.ds(pl.multiple_of(32 * ((r + k) % 4), 32), 32), :]


def misfit_kernel(place, own, r1, r2, r3, obs, rounded, share, buf):
    z = place[1]
    r = place[3]
    for i in range(8):
        s = own[i] + r1[i].astype(f32) + r2[i].astype(f32) + r3[i].astype(f32) - obs[i]
        rounded[i] = s.astype(bf16)

    for h in range(2):
        i = 2 * z + h
        s = own[i] + r1[i].astype(f32) + r2[i].astype(f32) + r3[i].astype(f32) - obs[i]
        for k in range(4):
            buf[pl.ds(pl.multiple_of(32 * ((r + k) % 4), 32), 32), :] = s[32 * k : 32 * k + 32, :]
        share[128 * h : 128 * h + 128, :] = buf[...].T


def bwd_kernel(rows, cols, cnt, place, *refs):
    mine = refs[0:4]
    other = refs[4:8]
    jac, g0, g1, g2, g3, jbuf, mis, acc, sems = refs[8:]
    live = cnt[0]
    x = place[0]
    core = place[2]
    n_chunks = (live + CHUNK - 1) // CHUNK
    total = jac.shape[0] // CHUNK

    def copy(i):
        return pltpu.make_async_copy(
            jac.at[pl.ds(i * CHUNK, CHUNK)], jbuf.at[pl.ds(i * CHUNK, CHUNK)], sems.at[i]
        )

    for i in range(total):
        @pl.when(i < n_chunks)
        def _():
            copy(i).start()

    acc[...] = jnp.zeros(acc.shape, f32)
    for k in range(4):
        b = 16 * ((x + k) % 4)
        for z in range(4):
            for h in range(2):
                mis[b + 4 * z + 2 * core + h] = mine[k][2 * z + h]
                mis[b + 4 * z + 2 * (1 - core) + h] = other[k][2 * z + h]

    def chunk(i, carry):
        copy(i).wait()
        for u in range(CHUNK // UNROLL):
            for v in range(UNROLL):
                s = i * CHUNK + u * UNROLL + v
                c = jnp.where(s < live, cols[s], 32)
                prod = jnp.dot(mis[rows[s]], jbuf[s], preferred_element_type=f32)
                acc[c] += prod
        return carry

    lax.fori_loop(0, n_chunks, chunk, 0)
    for k, out in enumerate((g0, g1, g2, g3)):
        for t in range(8):
            for q in range(4):
                out[t, 32 * q : 32 * q + 32, :] = acc[8 * q + t, 32 * k : 32 * k + 32, :].astype(out.dtype)


def sum_kernel(own, r1, r2, r3, grad, head, tail):
    for i in range(8):
        s = own[i] + r1[i].astype(f32) + r2[i].astype(f32) + r3[i].astype(f32)
        t = s.T
        grad[128 * i : 128 * i + 128, :] = t
        if i == 0:
            head[...] = t[:64, :]
        if i == 7:
            tail[...] = t[64:, :]


def wave_update(grad, nxt, prv, state_in, state, ext, levels):
    ln = lanes((64, 128))
    ext[0:64, :] = jnp.where(
        ln < 32, pltpu.roll(prv[...], 32, 1), pltpu.roll(grad[960:1024, :], 32, 1)
    )
    ext[64:1088, :] = grad[...]
    ext[1088:1152, :] = jnp.where(
        ln >= 96, pltpu.roll(nxt[...], 96, 1), pltpu.roll(grad[0:64, :], 96, 1)
    )
    ext[1152:1160, :] = jnp.zeros((8, 128), f32)
    src = ext
    for level in range(LEVELS):
        count = [576, 288, 144, 72, 40][level]
        front = 64 >> (level + 1)
        n = SEG_ROWS[level]
        base = SEG_OFF[level]
        e0 = src[pl.ds(0, count, stride=2), :]
        o0 = src[pl.ds(1, count, stride=2), :]
        e1 = src[pl.ds(2, count, stride=2), :]
        o1 = src[pl.ds(3, count, stride=2), :]
        smooth = low_pass[0] * e0 + low_pass[1] * o0 + low_pass[2] * e1 + low_pass[3] * o1
        detail = high_pass[0] * e0 + high_pass[1] * o0 + high_pass[2] * e1 + high_pass[3] * o1
        lead = min(front, 8)
        part = detail[front - lead : front + n, :]
        moved = state_in[base + 8 - lead : base + 8 + n, :] - step_length * part
        state[base + 8 - lead : base + 8 + n, :] = moved - jnp.clip(moved, -threshold, threshold)
        if lead < 8:
            state[base : base + 8 - lead, :] = jnp.zeros((8 - lead, 128), f32)
        if level < LEVELS - 1:
            dst = levels[level]
            dst[0:count, :] = smooth
            dst[count:, :] = jnp.zeros((dst.shape[0] - count, 128), f32)
            src = dst
        else:
            base = SEG_OFF[5]
            part = smooth[front - lead : front + n, :]
            state[base + 8 - lead : base + 8 + n, :] = (
                state_in[base + 8 - lead : base + 8 + n, :] - step_length * part
            )
            state[base : base + 8 - lead, :] = jnp.zeros((8 - lead, 128), f32)


WAVE_BUFS = [pltpu.VMEM((1160, 128), f32)] + [
    pltpu.VMEM((rows, 128), f32) for rows in (584, 296, 152, 88)
]


def wave_kernel(grad, nxt, prv, state_in, state, model_t, ext, l0, l1, l2, l3, *bufs):
    wave_update(grad, nxt, prv, state_in, state, ext, (l0, l1, l2, l3))
    synth_from(state, bufs, model_t)


def last_kernel(grad, nxt, prv, state_in, out, state, ext, l0, l1, l2, l3):
    wave_update(grad, nxt, prv, state_in, state, ext, (l0, l1, l2, l3))
    for g in range(6):
        n = SEG_ROWS[g]
        base = SEG_OFF[g]
        for q in range(4):
            out[COEF_OFF[g] + q * n : COEF_OFF[g] + (q + 1) * n, :] = state[
                base + 8 : base + 8 + n, 32 * q : 32 * q + 32
            ]


def from_ahead(x, axis, by):
    n = lax.axis_size(axis)
    return lax.ppermute(x, axis, [(i, (i - by) % n) for i in range(n)])


def to_ahead(x, axis, by):
    n = lax.axis_size(axis)
    return lax.ppermute(x, axis, [(i, (i + by) % n) for i in range(n)])


MP = ("x", "z", "core")


def along(x, by):
    return lax.ppermute(x, MP, [(i, (i + by) % 32) for i in range(32)])


def body(coeffs_start, observed, jacobian_tiles, tile_rows, tile_cols, tile_count):
    jac = jacobian_tiles[0, 0]
    rows = tile_rows[0, 0]
    cols = tile_cols[0, 0]
    cnt = tile_count[0]
    x, z, core, ray = (lax.axis_index(a) for a in ("x", "z", "core", "ray"))
    place = jnp.stack([x, z, core, ray]).astype(jnp.int32)
    tiles = sds((8, 128, 128), f32)
    tiles_b = sds((8, 128, 128), bf16)

    state, tails = call(
        init_kernel, "init", [VM], [sds((STATE_ROWS, 128), f32), sds((48, 128), f32)]
    )(coeffs_start)
    obs_rows = lax.dynamic_slice(
        observed.reshape(4, 4, 2, 256, 128), (x, 0, core, 0, 0), (1, 4, 1, 256, 128)
    ).reshape(4, 256, 128)
    (obs_t,) = call(
        obs_kernel, "obs", [SM, VM], [tiles], [pltpu.VMEM((128, 128), f32)]
    )(place, obs_rows)
    state, model_t = call(
        synth_kernel, "synth", [VM, VM], [sds((STATE_ROWS, 128), f32), tiles_b], SYNTH_BUFS
    )(state, along(tails, 1))

    n_slots = jac.shape[0]
    jac_scratch = pltpu.VMEM((n_slots, 128, 128), bf16)
    sems = pltpu.SemaphoreType.DMA((n_slots // CHUNK,))
    for sweep in range(ITERS):
        pieces = [model_t] + [from_ahead(model_t, "ray", k) for k in (1, 2, 3)]
        keep, send = call(
            fwd_kernel,
            "forward",
            [SM, SM, SM, SM, VM, VM, VM, VM, ANY],
            [sds((32, 128, 128), f32), sds((32, 128, 128), bf16)],
            [jac_scratch, pltpu.VMEM((32, 128, 128), bf16), pltpu.VMEM((65, 128, 128), f32), sems],
        )(rows, cols, cnt, place, *pieces, jac)
        got = to_ahead(send, "core", 1)
        own, s1, s2, s3 = call(
            split_kernel, "split", [SM, VM, VM], [tiles, tiles_b, tiles_b, tiles_b]
        )(place, keep, got)
        r = [to_ahead(s, "x", k + 1) for k, s in enumerate((s1, s2, s3))]
        own, sent = call(gather_kernel, "gather", [VM] * 4, [tiles, tiles_b])(own, *r)
        r = [to_ahead(sent, "z", k) for k in (1, 2, 3)]
        rounded, share = call(
            misfit_kernel,
            "misfit",
            [SM] + [VM] * 5,
            [tiles_b, sds((256, 128), f32)],
            [pltpu.VMEM((128, 128), f32)],
        )(place, own, *r, obs_t)
        mine = [rounded] + [from_ahead(rounded, "x", k) for k in (1, 2, 3)]
        other = [to_ahead(m, "core", 1) for m in mine]
        g0, g1, g2, g3 = call(
            bwd_kernel,
            "backward",
            [SM, SM, SM, SM] + [VM] * 8 + [ANY],
            [tiles, tiles_b, tiles_b, tiles_b],
            [jac_scratch, pltpu.VMEM((64, 128, 128), bf16), pltpu.VMEM((33, 128, 128), f32), sems],
        )(rows, cols, cnt, place, *mine, *other, jac)
        r = [to_ahead(g, "ray", k + 1) for k, g in enumerate((g1, g2, g3))]
        grad, head, tail = call(
            sum_kernel,
            "rays",
            [VM] * 4,
            [sds((1024, 128), f32), sds((64, 128), f32), sds((64, 128), f32)],
        )(g0, *r)
        nxt = along(head, -1)
        prv = along(tail, 1)
        if sweep < ITERS - 1:
            state, model_t = call(
                wave_kernel,
                "wave",
                [VM] * 4,
                [sds((STATE_ROWS, 128), f32), tiles_b],
                WAVE_BUFS + SYNTH_BUFS,
            )(grad, nxt, prv, state)
        else:
            (coeffs,) = call(
                last_kernel,
                "last",
                [VM] * 4,
                [sds((4096, 32), f32)],
                [pltpu.VMEM((STATE_ROWS, 128), f32)] + WAVE_BUFS,
            )(grad, nxt, prv, state)
    return (coeffs, share)


def solution(mesh):
    fine = Mesh(mesh.devices.reshape(4, 4, 4, 2), ("ray", "x", "z", "core"))
    placed = (
        P(MP, "ray"),
        P("ray", None),
        P("ray", MP, None, None, None),
        P("ray", MP, None),
        P("ray", MP, None),
        P("ray", MP),
    )
    return jax.shard_map(
        body,
        mesh=fine,
        in_specs=placed,
        out_specs=(P(MP, "ray"), P(("ray",) + MP, None)),
        check_vma=False,
    )
```

```python
import math

import jax
import jax.numpy as jnp
from jax import lax
from jax.experimental import pallas as pl
from jax.experimental.pallas import tpu as pltpu
from jax.sharding import Mesh, PartitionSpec as P

LEVELS = 5
ITERS = 2
TILE = 128
GROUP = 48
CHUNK = 16
ROW_BLOCKS = 64
CELL_TILES = 32

root_three = math.sqrt(3.0)
norm_factor = 4.0 * math.sqrt(2.0)
low_pass = [
    (1.0 + root_three) / norm_factor,
    (3.0 + root_three) / norm_factor,
    (3.0 - root_three) / norm_factor,
    (1.0 - root_three) / norm_factor,
]
high_pass = [low_pass[3], -low_pass[2], low_pass[1], -low_pass[0]]
step_length = 0.5
threshold = 0.1

f32 = jnp.float32
bf16 = jnp.bfloat16

SEG_ROWS = [512, 256, 128, 64, 32, 32]
SEG_OFF = [0]
for n in SEG_ROWS:
    SEG_OFF.append(SEG_OFF[-1] + 8 + n)
STATE_ROWS = SEG_OFF[-1]
COEF_OFF = [0, 2048, 3072, 3584, 3840, 3968]

VM = pl.BlockSpec(memory_space=pltpu.VMEM)
SM = pl.BlockSpec(memory_space=pltpu.SMEM)
ANY = pl.BlockSpec(memory_space=pl.ANY)


def sds(shape, dtype):
    return jax.ShapeDtypeStruct(shape, dtype)


def call(kernel, name, in_specs, outs, scratch=(), mib=40):
    return pl.pallas_call(
        kernel,
        name=name,
        in_specs=in_specs,
        out_specs=[VM] * len(outs),
        out_shape=outs,
        scratch_shapes=list(scratch),
        compiler_params=pltpu.CompilerParams(vmem_limit_bytes=mib * 1024 * 1024),
    )


def lanes(shape):
    return lax.broadcasted_iota(jnp.int32, shape, 1)


def init_kernel(coeffs, state, tails):
    for g in range(6):
        n = SEG_ROWS[g]
        base = SEG_OFF[g]
        parts = [coeffs[:, COEF_OFF[g] + q * n : COEF_OFF[g] + (q + 1) * n] for q in range(4)]
        packed = jnp.concatenate(parts, axis=0).T
        state[base + 8 : base + 8 + n, :] = packed
        last = packed[n - 8 : n, :]
        state[base : base + 8, :] = pltpu.roll(last, 32, 1)
        tails[8 * g : 8 * g + 8, :] = last


def axes(place, core):
    first = jnp.where(core == 0, place[1], place[0])
    second = jnp.where(core == 0, place[0], place[1])
    step = jnp.where(core == 0, 1, 4)
    return first, second, step, 5 - step


def tile_copies(jac, jbuf, sems, live):
    def copy(i):
        part = pl.ds(i * CHUNK, CHUNK)
        return pltpu.make_async_copy(jac.at[part], jbuf.at[part], sems.at[i])

    groups = (live + GROUP - 1) // GROUP
    per = GROUP // CHUNK

    for i in range(jac.shape[0] // CHUNK):
        @pl.when(i < groups * per)
        def _():
            copy(i).start()

    def arrive(g):
        for i in range(per):
            copy(g * per + i).wait()

    return groups, arrive


def synth_from(state, bufs, model):
    src = None
    for level in reversed(range(LEVELS)):
        n = SEG_ROWS[level]
        base = SEG_OFF[level]
        if src is None:
            sm = state[SEG_OFF[5] + 4 : SEG_OFF[5] + 8 + n, :]
            sp = state[SEG_OFF[5] + 3 : SEG_OFF[5] + 7 + n, :]
        else:
            sm = src[4 : 8 + n, :]
            sp = src[3 : 7 + n, :]
        dm = state[base + 4 : base + 8 + n, :]
        dp = state[base + 3 : base + 7 + n, :]
        even = low_pass[0] * sm + high_pass[0] * dm + low_pass[2] * sp + high_pass[2] * dp
        odd = low_pass[1] * sm + high_pass[1] * dm + low_pass[3] * sp + high_pass[3] * dp
        dst = bufs[level]
        dst[pl.ds(0, n + 4, stride=2), :] = even
        dst[pl.ds(1, n + 4, stride=2), :] = odd
        src = dst
    model[...] = src[8:1032, :].astype(bf16)


SYNTH_BUFS = [pltpu.VMEM((8 + 2 * SEG_ROWS[l], 128), f32) for l in range(LEVELS)]


def synth_kernel(state_in, recv, state, model, *bufs):
    state[...] = state_in[...]
    for g in range(6):
        base = SEG_OFF[g]
        own = state_in[base : base + 8, :]
        got = pltpu.roll(recv[8 * g : 8 * g + 8, :], 32, 1)
        state[base : base + 8, :] = jnp.where(lanes((8, 128)) < 32, got, own)
    synth_from(state, bufs, model)


def fwd_kernel(rows, cols, cnt, place, p0, p1, p2, p3, jac, keep, send, jbuf, model, acc, sems):
    live = cnt[0]
    core = place[2]
    groups, arrive = tile_copies(jac, jbuf, sems, live)
    acc[...] = jnp.zeros(acc.shape, f32)
    for c in range(CELL_TILES):
        q, t = c // 8, c % 8
        model[c] = jnp.concatenate(
            [p[128 * t : 128 * t + 128, 32 * q : 32 * q + 32] for p in (p0, p1, p2, p3)], axis=1
        )

    def group(g, carry):
        arrive(g)
        for v in range(GROUP):
            s = g * GROUP + v
            r = jnp.where(s < live, rows[s], ROW_BLOCKS)
            acc[r] += jnp.dot(jbuf[s], model[cols[s]], preferred_element_type=f32)
        return carry

    lax.fori_loop(0, groups, group, 0)
    for xz in range(16):
        for h in range(2):
            keep[2 * xz + h] = acc[4 * xz + 2 * core + h]
            send[2 * xz + h] = acc[4 * xz + 2 * (1 - core) + h].astype(bf16)


def split_kernel(place, keep, recv, own, s1, s2, s3):
    first, second, step, other = axes(place, place[2])
    for k, out in enumerate((own, s1, s2, s3)):
        for e in range(4):
            for h in range(2):
                b = 2 * (step * ((first + k) % 4) + other * e) + h
                out[2 * e + h] = (keep[b] + recv[b].astype(f32)).astype(out.dtype)


def gather_kernel(own, r1, r2, r3, total, sent):
    for i in range(8):
        s = own[i] + r1[i].astype(f32) + r2[i].astype(f32) + r3[i].astype(f32)
        total[i] = s
        sent[i] = s.astype(bf16)


def misfit_tile(own, r1, r2, r3, obs, i):
    return own[i] + r1[i].astype(f32) + r2[i].astype(f32) + r3[i].astype(f32) - obs[i]


def obs_kernel(place, obs, out):
    back = (128 - 32 * place[3]) % 128
    for i in range(8):
        out[i] = pltpu.roll(obs[i // 2, 128 * (i % 2) : 128 * (i % 2) + 128, :], back, 1)


def misfit_kernel(own, r1, r2, r3, obs, rounded):
    for i in range(8):
        rounded[i] = misfit_tile(own, r1, r2, r3, obs, i).T.astype(bf16)


def share_kernel(place, own, r1, r2, r3, obs, share):
    for h in range(2):
        tile = misfit_tile(own, r1, r2, r3, obs, 2 * axes(place, place[2])[1] + h)
        share[128 * h : 128 * h + 128, :] = pltpu.roll(tile, 32 * place[3], 1)


def bwd_kernel(rows, cols, cnt, place, *refs):
    jac, g0, g1, g2, g3, jbuf, mis, acc, sems = refs[8:]
    live = cnt[0]
    core = place[2]
    groups, arrive = tile_copies(jac, jbuf, sems, live)
    acc[...] = jnp.zeros(acc.shape, f32)
    for pieces, c in ((refs[0:4], core), (refs[4:8], 1 - core)):
        first, second, step, other = axes(place, c)
        for k in range(4):
            b = 4 * step * ((first + k) % 4) + 2 * c
            for e in range(4):
                for h in range(2):
                    mis[b + 4 * other * e + h] = pieces[k][2 * e + h]

    def group(g, carry):
        arrive(g)
        for v in range(GROUP):
            s = g * GROUP + v
            c = jnp.where(s < live, cols[s], CELL_TILES)
            acc[c] += jnp.dot(mis[rows[s]], jbuf[s], preferred_element_type=f32)
        return carry

    lax.fori_loop(0, groups, group, 0)
    for k, out in enumerate((g0, g1, g2, g3)):
        for t in range(8):
            for q in range(4):
                out[t, 32 * q : 32 * q + 32, :] = acc[8 * q + t, 32 * k : 32 * k + 32, :].astype(out.dtype)


def sum_kernel(own, r1, r2, r3, grad, head, tail):
    for i in range(8):
        s = own[i] + r1[i].astype(f32) + r2[i].astype(f32) + r3[i].astype(f32)
        t = s.T
        grad[128 * i : 128 * i + 128, :] = t
        if i == 0:
            head[...] = t[:64, :]
        if i == 7:
            tail[...] = t[64:, :]


def wave_update(grad, nxt, prv, state_in, state, ext, levels):
    ln = lanes((64, 128))
    ext[0:64, :] = jnp.where(
        ln < 32, pltpu.roll(prv[...], 32, 1), pltpu.roll(grad[960:1024, :], 32, 1)
    )
    ext[64:1088, :] = grad[...]
    ext[1088:1152, :] = jnp.where(
        ln >= 96, pltpu.roll(nxt[...], 96, 1), pltpu.roll(grad[0:64, :], 96, 1)
    )
    ext[1152:1160, :] = jnp.zeros((8, 128), f32)
    src = ext
    for level in range(LEVELS):
        count = [576, 288, 144, 72, 40][level]
        front = 64 >> (level + 1)
        n = SEG_ROWS[level]
        base = SEG_OFF[level]
        e0 = src[pl.ds(0, count, stride=2), :]
        o0 = src[pl.ds(1, count, stride=2), :]
        e1 = src[pl.ds(2, count, stride=2), :]
        o1 = src[pl.ds(3, count, stride=2), :]
        smooth = low_pass[0] * e0 + low_pass[1] * o0 + low_pass[2] * e1 + low_pass[3] * o1
        detail = high_pass[0] * e0 + high_pass[1] * o0 + high_pass[2] * e1 + high_pass[3] * o1
        lead = min(front, 8)
        part = detail[front - lead : front + n, :]
        moved = state_in[base + 8 - lead : base + 8 + n, :] - step_length * part
        state[base + 8 - lead : base + 8 + n, :] = moved - jnp.clip(moved, -threshold, threshold)
        if lead < 8:
            state[base : base + 8 - lead, :] = jnp.zeros((8 - lead, 128), f32)
        if level < LEVELS - 1:
            dst = levels[level]
            dst[0:count, :] = smooth
            dst[count:, :] = jnp.zeros((dst.shape[0] - count, 128), f32)
            src = dst
        else:
            base = SEG_OFF[5]
            part = smooth[front - lead : front + n, :]
            state[base + 8 - lead : base + 8 + n, :] = (
                state_in[base + 8 - lead : base + 8 + n, :] - step_length * part
            )
            state[base : base + 8 - lead, :] = jnp.zeros((8 - lead, 128), f32)


WAVE_BUFS = [pltpu.VMEM((1160, 128), f32)] + [
    pltpu.VMEM((rows, 128), f32) for rows in (584, 296, 152, 88)
]


def wave_kernel(grad, nxt, prv, state_in, state, model, ext, l0, l1, l2, l3, *bufs):
    wave_update(grad, nxt, prv, state_in, state, ext, (l0, l1, l2, l3))
    synth_from(state, bufs, model)


def last_kernel(grad, nxt, prv, state_in, out, state, ext, l0, l1, l2, l3):
    wave_update(grad, nxt, prv, state_in, state, ext, (l0, l1, l2, l3))
    for g in range(6):
        n = SEG_ROWS[g]
        base = SEG_OFF[g]
        tile = state[base + 8 : base + 8 + n, :].T
        for q in range(4):
            out[:, COEF_OFF[g] + q * n : COEF_OFF[g] + (q + 1) * n] = tile[32 * q : 32 * q + 32, :]


def from_ahead(x, axis, by):
    n = lax.axis_size(axis)
    return lax.ppermute(x, axis, [(i, (i - by) % n) for i in range(n)])


def to_ahead(x, axis, by):
    n = lax.axis_size(axis)
    return lax.ppermute(x, axis, [(i, (i + by) % n) for i in range(n)])


def by_core(x, stage, by):
    pairs = []
    for i in range(4):
        for j in range(4):
            for c in range(2):
                to = (i, (j + by) % 4) if c == stage else ((i + by) % 4, j)
                pairs.append((8 * i + 2 * j + c, 8 * to[0] + 2 * to[1] + c))
    return lax.ppermute(x, MP, pairs)


MP = ("x", "z", "core")


def along(x, by):
    return lax.ppermute(x, MP, [(i, (i + by) % 32) for i in range(32)])


def body(coeffs_start, observed, jacobian_tiles, tile_rows, tile_cols, tile_count):
    jac = jacobian_tiles[0, 0]
    rows = tile_rows[0, 0]
    cols = tile_cols[0, 0]
    cnt = tile_count[0]
    n_slots = jac.shape[0]
    x, z, core, ray = (lax.axis_index(a) for a in ("x", "z", "core", "ray"))
    place = jnp.stack([x, z, core, ray]).astype(jnp.int32)
    tiles = sds((8, 128, 128), f32)
    tiles_b = sds((8, 128, 128), bf16)
    flat_b = sds((1024, 128), bf16)

    state, tails = call(
        init_kernel, "init", [VM], [sds((STATE_ROWS, 128), f32), sds((48, 128), f32)]
    )(coeffs_start.T)
    obs_all = observed.reshape(4, 4, 2, 256, 128)
    obs_rows = lax.cond(
        core == 0,
        lambda a: lax.dynamic_slice(a, (0, z, 0, 0, 0), (4, 1, 1, 256, 128)).reshape(4, 256, 128),
        lambda a: lax.dynamic_slice(a, (x, 0, 1, 0, 0), (1, 4, 1, 256, 128)).reshape(4, 256, 128),
        obs_all,
    )
    (obs_t,) = call(obs_kernel, "obs", [SM, VM], [tiles])(place, obs_rows)
    state, model = call(
        synth_kernel, "synth", [VM, VM], [sds((STATE_ROWS, 128), f32), flat_b], SYNTH_BUFS
    )(state, along(tails, 1))

    jac_scratch = pltpu.VMEM((n_slots, TILE, TILE), bf16)
    sems = pltpu.SemaphoreType.DMA((n_slots // CHUNK,))
    for sweep in range(ITERS):
        pieces = [model] + [from_ahead(model, "ray", k) for k in (1, 2, 3)]
        keep, send = call(
            fwd_kernel,
            "forward",
            [SM, SM, SM, SM, VM, VM, VM, VM, ANY],
            [sds((32, 128, 128), f32), sds((32, 128, 128), bf16)],
            [jac_scratch, pltpu.VMEM((32, 128, 128), bf16), pltpu.VMEM((65, 128, 128), f32), sems],
        )(rows, cols, cnt, place, *pieces, jac)
        got = to_ahead(send, "core", 1)
        own, s1, s2, s3 = call(
            split_kernel, "split", [SM, VM, VM], [tiles, tiles_b, tiles_b, tiles_b]
        )(place, keep, got)
        r = [by_core(s, 0, k + 1) for k, s in enumerate((s1, s2, s3))]
        own, sent = call(gather_kernel, "gather", [VM] * 4, [tiles, tiles_b])(own, *r)
        r = [by_core(sent, 1, k) for k in (1, 2, 3)]
        (rounded,) = call(misfit_kernel, "misfit", [VM] * 5, [tiles_b])(own, *r, obs_t)
        if sweep == ITERS - 1:
            (share,) = call(share_kernel, "share", [SM] + [VM] * 5, [sds((256, 128), f32)])(
                place, own, *r, obs_t
            )
        mine = [rounded] + [by_core(rounded, 0, -k) for k in (1, 2, 3)]
        other = [to_ahead(m, "core", 1) for m in mine]
        g0, g1, g2, g3 = call(
            bwd_kernel,
            "backward",
            [SM, SM, SM, SM] + [VM] * 8 + [ANY],
            [tiles, tiles_b, tiles_b, tiles_b],
            [jac_scratch, pltpu.VMEM((64, 128, 128), bf16), pltpu.VMEM((33, 128, 128), f32), sems],
        )(rows, cols, cnt, place, *mine, *other, jac)
        r = [to_ahead(g, "ray", k + 1) for k, g in enumerate((g1, g2, g3))]
        grad, head, tail = call(
            sum_kernel,
            "rays",
            [VM] * 4,
            [sds((1024, 128), f32), sds((64, 128), f32), sds((64, 128), f32)],
        )(g0, *r)
        nxt = along(head, -1)
        prv = along(tail, 1)
        if sweep < ITERS - 1:
            state, model = call(
                wave_kernel,
                "wave",
                [VM] * 4,
                [sds((STATE_ROWS, 128), f32), flat_b],
                WAVE_BUFS + SYNTH_BUFS,
            )(grad, nxt, prv, state)
        else:
            (coeffs,) = call(
                last_kernel,
                "last",
                [VM] * 4,
                [sds((32, 4096), f32)],
                [pltpu.VMEM((STATE_ROWS, 128), f32)] + WAVE_BUFS,
            )(grad, nxt, prv, state)
    return (coeffs.T, share)


def solution(mesh):
    fine = Mesh(mesh.devices.reshape(4, 4, 4, 2), ("ray", "x", "z", "core"))
    placed = (
        P(MP, "ray"),
        P("ray", None),
        P("ray", MP, None, None, None),
        P("ray", MP, None),
        P("ray", MP, None),
        P("ray", MP),
    )
    return jax.shard_map(
        body,
        mesh=fine,
        in_specs=placed,
        out_specs=(P(MP, "ray"), P(("ray",) + MP, None)),
        check_vma=False,
    )
```

```python
import math

import jax
import jax.numpy as jnp
from jax import lax
from jax.experimental import pallas as pl
from jax.experimental.pallas import tpu as pltpu
from jax.sharding import Mesh, PartitionSpec as P


LEVELS = 5
ITERS = 2
TILE = 128
GROUP = 48
CHUNK = 16
ROW_BLOCKS = 64
CELL_TILES = 32


root_three = math.sqrt(3.0)
norm_factor = 4.0 * math.sqrt(2.0)
low_pass = [
    (1.0 + root_three) / norm_factor,
    (3.0 + root_three) / norm_factor,
    (3.0 - root_three) / norm_factor,
    (1.0 - root_three) / norm_factor,
]
high_pass = [low_pass[3], -low_pass[2], low_pass[1], -low_pass[0]]
step_length = 0.5
threshold = 0.1

f32 = jnp.float32
bf16 = jnp.bfloat16

SEG_ROWS = [512, 256, 128, 64, 32, 32]
SEG_OFF = [0]
for n in SEG_ROWS:
    SEG_OFF.append(SEG_OFF[-1] + 8 + n)
STATE_ROWS = SEG_OFF[-1]
COEF_OFF = [0, 2048, 3072, 3584, 3840, 3968]

VM = pl.BlockSpec(memory_space=pltpu.VMEM)
SM = pl.BlockSpec(memory_space=pltpu.SMEM)
ANY = pl.BlockSpec(memory_space=pl.ANY)


def sds(shape, dtype):
    return jax.ShapeDtypeStruct(shape, dtype)


def call(kernel, in_specs, outs, scratch=(), mib=40):
    return pl.pallas_call(
        kernel,
        in_specs=in_specs,
        out_specs=[VM] * len(outs),
        out_shape=outs,
        scratch_shapes=list(scratch),
        compiler_params=pltpu.CompilerParams(vmem_limit_bytes=mib * 1024 * 1024),
    )


def lanes(shape):
    return lax.broadcasted_iota(jnp.int32, shape, 1)


def init_kernel(coeffs, state, tails):
    for g in range(6):
        n = SEG_ROWS[g]
        base = SEG_OFF[g]
        parts = [coeffs[:, COEF_OFF[g] + q * n : COEF_OFF[g] + (q + 1) * n] for q in range(4)]
        packed = jnp.concatenate(parts, axis=0).T
        state[base + 8 : base + 8 + n, :] = packed
        last = packed[n - 8 : n, :]
        state[base : base + 8, :] = pltpu.roll(last, 32, 1)
        tails[8 * g : 8 * g + 8, :] = last


def axes(place, core):
    first = jnp.where(core == 0, place[1], place[0])
    second = jnp.where(core == 0, place[0], place[1])
    step = jnp.where(core == 0, 1, 4)
    return first, second, step, 5 - step


def tile_copies(jac, jbuf, sems, live):
    def copy(i):
        part = pl.ds(i * CHUNK, CHUNK)
        return pltpu.make_async_copy(jac.at[part], jbuf.at[part], sems.at[i])

    groups = (live + GROUP - 1) // GROUP
    per = GROUP // CHUNK

    for i in range(jac.shape[0] // CHUNK):
        @pl.when(i < groups * per)
        def _():
            copy(i).start()

    def arrive(g):
        for i in range(per):
            copy(g * per + i).wait()

    return groups, arrive


def synth_from(state, bufs, model):
    src = None
    for level in reversed(range(LEVELS)):
        n = SEG_ROWS[level]
        base = SEG_OFF[level]
        if src is None:
            sm = state[SEG_OFF[5] + 4 : SEG_OFF[5] + 8 + n, :]
            sp = state[SEG_OFF[5] + 3 : SEG_OFF[5] + 7 + n, :]
        else:
            sm = src[4 : 8 + n, :]
            sp = src[3 : 7 + n, :]
        dm = state[base + 4 : base + 8 + n, :]
        dp = state[base + 3 : base + 7 + n, :]
        even = low_pass[0] * sm + high_pass[0] * dm + low_pass[2] * sp + high_pass[2] * dp
        odd = low_pass[1] * sm + high_pass[1] * dm + low_pass[3] * sp + high_pass[3] * dp
        dst = bufs[level]
        dst[pl.ds(0, n + 4, stride=2), :] = even
        dst[pl.ds(1, n + 4, stride=2), :] = odd
        src = dst
    model[...] = src[8:1032, :].astype(bf16)


SYNTH_BUFS = [pltpu.VMEM((8 + 2 * SEG_ROWS[l], 128), f32) for l in range(LEVELS)]


def early_kernel(state, model, *bufs):
    synth_from(state, bufs, model)


def synth_kernel(state_in, recv, state, fix, *scratch):
    state[...] = state_in[...]
    for g in range(6):
        base = SEG_OFF[g]
        own = state_in[base : base + 8, :]
        got = pltpu.roll(recv[8 * g : 8 * g + 8, :], 32, 1)
        state[base : base + 8, :] = jnp.where(lanes((8, 128)) < 32, got, own)
    model = scratch[-1]
    synth_from(state, scratch[:-1], model)
    fix[...] = model[0:128, :]


def first_kernel(rows, cols, cnt, place, f0, f1, f2, f3, *refs):
    fwd_kernel(rows, cols, cnt, place, *refs, fixes=(f0, f1, f2, f3))


def fwd_kernel(
    rows, cols, cnt, place, p0, p1, p2, p3, jac, keep, send, jbuf, model, acc, sems, fixes=None
):
    live = cnt[0]
    core = place[2]
    groups, arrive = tile_copies(jac, jbuf, sems, live)
    acc[...] = jnp.zeros(acc.shape, f32)
    for c in range(CELL_TILES):
        q, t = c // 8, c % 8
        pieces = fixes if c == 0 and fixes else (p0, p1, p2, p3)
        model[c] = jnp.concatenate(
            [p[128 * t : 128 * t + 128, 32 * q : 32 * q + 32] for p in pieces], axis=1
        )

    def group(g, carry):
        arrive(g)
        for v in range(GROUP):
            s = g * GROUP + v
            r = jnp.where(s < live, rows[s], ROW_BLOCKS)
            acc[r] += jnp.dot(jbuf[s], model[cols[s]], preferred_element_type=f32)
        return carry

    lax.fori_loop(0, groups, group, 0)
    for xz in range(16):
        for h in range(2):
            keep[2 * xz + h] = acc[4 * xz + 2 * core + h]
            send[2 * xz + h] = acc[4 * xz + 2 * (1 - core) + h].astype(bf16)


def split_kernel(place, keep, recv, own, s1, s2, s3):
    first, _, step, other = axes(place, place[2])
    for k, out in enumerate((own, s1, s2, s3)):
        for e in range(4):
            for h in range(2):
                b = 2 * (step * ((first + k) % 4) + other * e) + h
                out[2 * e + h] = (keep[b] + recv[b].astype(f32)).astype(out.dtype)


def gather_kernel(own, r1, r2, r3, total, sent):
    for i in range(8):
        s = own[i] + r1[i].astype(f32) + r2[i].astype(f32) + r3[i].astype(f32)
        total[i] = s
        sent[i] = s.astype(bf16)


def misfit_tile(own, r1, r2, r3, obs, i):
    return own[i] + r1[i].astype(f32) + r2[i].astype(f32) + r3[i].astype(f32) - obs[i]


def obs_kernel(place, obs, out):
    back = (128 - 32 * place[3]) % 128
    for i in range(8):
        out[i] = pltpu.roll(obs[i // 2, 128 * (i % 2) : 128 * (i % 2) + 128, :], back, 1)


def misfit_kernel(own, r1, r2, r3, obs, rounded):
    for i in range(8):
        rounded[i] = misfit_tile(own, r1, r2, r3, obs, i).T.astype(bf16)


def share_kernel(place, own, r1, r2, r3, obs, share):
    for h in range(2):
        tile = misfit_tile(own, r1, r2, r3, obs, 2 * axes(place, place[2])[1] + h)
        share[128 * h : 128 * h + 128, :] = pltpu.roll(tile, 32 * place[3], 1)


def bwd_kernel(rows, cols, cnt, place, *refs):
    jac, g0, g1, g2, g3, e0, e1, e2, e3, jbuf, mis, acc, sems = refs[8:]
    live = cnt[0]
    core = place[2]
    groups, arrive = tile_copies(jac, jbuf, sems, live)
    acc[...] = jnp.zeros(acc.shape, f32)
    for pieces, c in ((refs[0:4], core), (refs[4:8], 1 - core)):
        first, _, step, other = axes(place, c)
        for k in range(4):
            b = 4 * step * ((first + k) % 4) + 2 * c
            for e in range(4):
                for h in range(2):
                    mis[b + 4 * other * e + h] = pieces[k][2 * e + h]

    def group(g, carry):
        arrive(g)
        for v in range(GROUP):
            s = g * GROUP + v
            c = jnp.where(s < live, cols[s], CELL_TILES)
            acc[c] += jnp.dot(mis[rows[s]], jbuf[s], preferred_element_type=f32)
        return carry

    lax.fori_loop(0, groups, group, 0)
    for k, out in enumerate((e0, e1, e2, e3)):
        part = slice(32 * k, 32 * k + 32)
        edge = jnp.where(lanes((32, 128)) < 64, acc[0, part, :], acc[CELL_TILES - 1, part, :])
        out[...] = edge.astype(out.dtype)
    for k, out in enumerate((g0, g1, g2, g3)):
        for t in range(8):
            for q in range(4):
                out[t, 32 * q : 32 * q + 32, :] = acc[8 * q + t, 32 * k : 32 * k + 32, :].astype(out.dtype)


def edge_kernel(own, r1, r2, r3, edge):
    edge[...] = own[...] + r1[...].astype(f32) + r2[...].astype(f32) + r3[...].astype(f32)


def wave_update(own, r1, r2, r3, nxt, prv, state_in, state, ext, levels):
    for i in range(8):
        s = own[i] + r1[i].astype(f32) + r2[i].astype(f32) + r3[i].astype(f32)
        ext[64 + 128 * i : 192 + 128 * i, :] = s.T
    ln = lanes((64, 128))
    near = jnp.concatenate([prv[...], jnp.zeros((64, 128), f32), nxt[...]], axis=0).T
    ext[0:64, :] = jnp.where(ln < 32, near[64:, :], pltpu.roll(ext[1024:1088, :], 32, 1))
    ext[1088:1152, :] = jnp.where(ln >= 96, near[:64, :], pltpu.roll(ext[64:128, :], 96, 1))
    ext[1152:1160, :] = jnp.zeros((8, 128), f32)
    src = ext
    for level in range(LEVELS):
        count = [576, 288, 144, 72, 40][level]
        front = 64 >> (level + 1)
        n = SEG_ROWS[level]
        base = SEG_OFF[level]
        e0 = src[pl.ds(0, count, stride=2), :]
        o0 = src[pl.ds(1, count, stride=2), :]
        e1 = src[pl.ds(2, count, stride=2), :]
        o1 = src[pl.ds(3, count, stride=2), :]
        smooth = low_pass[0] * e0 + low_pass[1] * o0 + low_pass[2] * e1 + low_pass[3] * o1
        detail = high_pass[0] * e0 + high_pass[1] * o0 + high_pass[2] * e1 + high_pass[3] * o1
        lead = min(front, 8)
        part = detail[front - lead : front + n, :]
        moved = state_in[base + 8 - lead : base + 8 + n, :] - step_length * part
        state[base + 8 - lead : base + 8 + n, :] = moved - jnp.clip(moved, -threshold, threshold)
        if lead < 8:
            state[base : base + 8 - lead, :] = jnp.zeros((8 - lead, 128), f32)
        if level < LEVELS - 1:
            dst = levels[level]
            dst[0:count, :] = smooth
            dst[count:, :] = jnp.zeros((dst.shape[0] - count, 128), f32)
            src = dst
        else:
            base = SEG_OFF[5]
            part = smooth[front - lead : front + n, :]
            state[base + 8 - lead : base + 8 + n, :] = (
                state_in[base + 8 - lead : base + 8 + n, :] - step_length * part
            )
            state[base : base + 8 - lead, :] = jnp.zeros((8 - lead, 128), f32)


WAVE_BUFS = [pltpu.VMEM((1160, 128), f32)] + [
    pltpu.VMEM((rows, 128), f32) for rows in (584, 296, 152, 88)
]


def wave_kernel(
    own, r1, r2, r3, nxt, prv, state_in, state, model, ext, l0, l1, l2, l3, *bufs
):
    wave_update(own, r1, r2, r3, nxt, prv, state_in, state, ext, (l0, l1, l2, l3))
    synth_from(state, bufs, model)


def last_kernel(own, r1, r2, r3, nxt, prv, state_in, out, state, ext, l0, l1, l2, l3):
    wave_update(own, r1, r2, r3, nxt, prv, state_in, state, ext, (l0, l1, l2, l3))
    for g in range(6):
        n = SEG_ROWS[g]
        base = SEG_OFF[g]
        tile = state[base + 8 : base + 8 + n, :].T
        for q in range(4):
            out[:, COEF_OFF[g] + q * n : COEF_OFF[g] + (q + 1) * n] = tile[32 * q : 32 * q + 32, :]


def from_ahead(x, axis, by):
    n = lax.axis_size(axis)
    return lax.ppermute(x, axis, [(i, (i - by) % n) for i in range(n)])


def to_ahead(x, axis, by):
    n = lax.axis_size(axis)
    return lax.ppermute(x, axis, [(i, (i + by) % n) for i in range(n)])


def by_core(x, stage, by):
    pairs = []
    for i in range(4):
        for j in range(4):
            for c in range(2):
                to = (i, (j + by) % 4) if c == stage else ((i + by) % 4, j)
                pairs.append((8 * i + 2 * j + c, 8 * to[0] + 2 * to[1] + c))
    return lax.ppermute(x, MP, pairs)


MP = ("x", "z", "core")


def along(x, by):
    return lax.ppermute(x, MP, [(i, (i + by) % 32) for i in range(32)])


def body(coeffs_start, observed, jacobian_tiles, tile_rows, tile_cols, tile_count):
    jac = jacobian_tiles[0, 0]
    rows = tile_rows[0, 0]
    cols = tile_cols[0, 0]
    cnt = tile_count[0]
    n_slots = jac.shape[0]
    x, z, core, ray = (lax.axis_index(a) for a in ("x", "z", "core", "ray"))
    place = jnp.stack([x, z, core, ray]).astype(jnp.int32)
    tiles = sds((8, 128, 128), f32)
    tiles_b = sds((8, 128, 128), bf16)
    flat_b = sds((1024, 128), bf16)

    state, tails = call(
        init_kernel, [VM], [sds((STATE_ROWS, 128), f32), sds((48, 128), f32)]
    )(coeffs_start.T)
    obs_all = observed.reshape(4, 4, 2, 256, 128)
    obs_rows = lax.cond(
        core == 0,
        lambda a: lax.dynamic_slice(a, (0, z, 0, 0, 0), (4, 1, 1, 256, 128)).reshape(4, 256, 128),
        lambda a: lax.dynamic_slice(a, (x, 0, 1, 0, 0), (1, 4, 1, 256, 128)).reshape(4, 256, 128),
        obs_all,
    )
    (obs_t,) = call(obs_kernel, [SM, VM], [tiles])(place, obs_rows)
    recv = along(tails, 1)
    (model,) = call(early_kernel, [VM], [flat_b], SYNTH_BUFS)(state)
    state, fix = call(
        synth_kernel,
        [VM, VM],
        [sds((STATE_ROWS, 128), f32), sds((128, 128), bf16)],
        SYNTH_BUFS + [pltpu.VMEM((1024, 128), bf16)],
    )(state, recv)

    jac_scratch = pltpu.VMEM((n_slots, TILE, TILE), bf16)
    sems = pltpu.SemaphoreType.DMA((n_slots // CHUNK,))
    for sweep in range(ITERS):
        pieces = [model] + [from_ahead(model, "ray", k) for k in (1, 2, 3)]
        fixes = []
        if sweep == 0:
            fixes = [fix] + [from_ahead(fix, "ray", k) for k in (1, 2, 3)]
        keep, send = call(
            fwd_kernel if sweep else first_kernel,
            [SM] * 4 + [VM] * (4 + len(fixes)) + [ANY],
            [sds((32, 128, 128), f32), sds((32, 128, 128), bf16)],
            [jac_scratch, pltpu.VMEM((32, 128, 128), bf16), pltpu.VMEM((65, 128, 128), f32), sems],
        )(rows, cols, cnt, place, *fixes, *pieces, jac)
        got = to_ahead(send, "core", 1)
        own, s1, s2, s3 = call(
            split_kernel, [SM, VM, VM], [tiles, tiles_b, tiles_b, tiles_b]
        )(place, keep, got)
        r = [by_core(s, 0, k + 1) for k, s in enumerate((s1, s2, s3))]
        own, sent = call(gather_kernel, [VM] * 4, [tiles, tiles_b])(own, *r)
        r = [by_core(sent, 1, k) for k in (1, 2, 3)]
        (rounded,) = call(misfit_kernel, [VM] * 5, [tiles_b])(own, *r, obs_t)
        if sweep == ITERS - 1:
            (share,) = call(share_kernel, [SM] + [VM] * 5, [sds((256, 128), f32)])(
                place, own, *r, obs_t
            )
        mine = [rounded] + [by_core(rounded, 0, -k) for k in (1, 2, 3)]
        other = [to_ahead(m, "core", 1) for m in mine]
        edge, edge_b = sds((32, 128), f32), sds((32, 128), bf16)
        g0, g1, g2, g3, e0, e1, e2, e3 = call(
            bwd_kernel,
            [SM, SM, SM, SM] + [VM] * 8 + [ANY],
            [tiles, tiles_b, tiles_b, tiles_b, edge, edge_b, edge_b, edge_b],
            [jac_scratch, pltpu.VMEM((64, 128, 128), bf16), pltpu.VMEM((33, 128, 128), f32), sems],
        )(rows, cols, cnt, place, *mine, *other, jac)
        r = [to_ahead(e, "ray", k + 1) for k, e in enumerate((e1, e2, e3))]
        (near,) = call(edge_kernel, [VM] * 4, [edge])(e0, *r)
        nxt = along(near, -1)
        prv = along(near, 1)
        r = [to_ahead(g, "ray", k + 1) for k, g in enumerate((g1, g2, g3))]
        if sweep < ITERS - 1:
            state, model = call(
                wave_kernel, [VM] * 7, [sds((STATE_ROWS, 128), f32), flat_b], WAVE_BUFS + SYNTH_BUFS
            )(g0, *r, nxt, prv, state)
        else:
            (coeffs,) = call(
                last_kernel,
                [VM] * 7,
                [sds((32, 4096), f32)],
                [pltpu.VMEM((STATE_ROWS, 128), f32)] + WAVE_BUFS,
            )(g0, *r, nxt, prv, state)
    return (coeffs.T, share)


def solution(mesh):
    fine = Mesh(mesh.devices.reshape(4, 4, 4, 2), ("ray", "x", "z", "core"))
    placed = (
        P(MP, "ray"),
        P("ray", None),
        P("ray", MP, None, None, None),
        P("ray", MP, None),
        P("ray", MP, None),
        P("ray", MP),
    )
    return jax.shard_map(
        body,
        mesh=fine,
        in_specs=placed,
        out_specs=(P(MP, "ray"), P(("ray",) + MP, None)),
        check_vma=False,
    )
```

```python
import math

import jax
import jax.numpy as jnp
from jax import lax
from jax.experimental import pallas as pl
from jax.experimental.pallas import tpu as pltpu
from jax.sharding import Mesh, PartitionSpec as P


LEVELS = 5
ITERS = 2
TILE = 128
GROUP = 48
CHUNK = 16
ROW_BLOCKS = 64
CELL_TILES = 32


root_three = math.sqrt(3.0)
norm_factor = 4.0 * math.sqrt(2.0)
low_pass = [
    (1.0 + root_three) / norm_factor,
    (3.0 + root_three) / norm_factor,
    (3.0 - root_three) / norm_factor,
    (1.0 - root_three) / norm_factor,
]
high_pass = [low_pass[3], -low_pass[2], low_pass[1], -low_pass[0]]
step_length = 0.5
threshold = 0.1

f32 = jnp.float32
bf16 = jnp.bfloat16

SEG_ROWS = [512, 256, 128, 64, 32, 32]
SEG_OFF = [0]
for n in SEG_ROWS:
    SEG_OFF.append(SEG_OFF[-1] + 8 + n)
STATE_ROWS = SEG_OFF[-1]
COEF_OFF = [0, 2048, 3072, 3584, 3840, 3968]

VM = pl.BlockSpec(memory_space=pltpu.VMEM)
SM = pl.BlockSpec(memory_space=pltpu.SMEM)
ANY = pl.BlockSpec(memory_space=pl.ANY)


def sds(shape, dtype):
    return jax.ShapeDtypeStruct(shape, dtype)


def call(kernel, in_specs, outs, scratch=(), mib=40):
    return pl.pallas_call(
        kernel,
        in_specs=in_specs,
        out_specs=[VM] * len(outs),
        out_shape=outs,
        scratch_shapes=list(scratch),
        compiler_params=pltpu.CompilerParams(vmem_limit_bytes=mib * 1024 * 1024),
    )


def lanes(shape):
    return lax.broadcasted_iota(jnp.int32, shape, 1)


def init_kernel(coeffs, state, tails):
    for g in range(6):
        n = SEG_ROWS[g]
        base = SEG_OFF[g]
        parts = [coeffs[:, COEF_OFF[g] + q * n : COEF_OFF[g] + (q + 1) * n] for q in range(4)]
        packed = jnp.concatenate(parts, axis=0).T
        state[base + 8 : base + 8 + n, :] = packed
        last = packed[n - 8 : n, :]
        state[base : base + 8, :] = pltpu.roll(last, 32, 1)
        tails[8 * g : 8 * g + 8, :] = last


def axes(place, core):
    first = jnp.where(core == 0, place[1], place[0])
    second = jnp.where(core == 0, place[0], place[1])
    step = jnp.where(core == 0, 1, 4)
    return first, second, step, 5 - step


def tile_copies(jac, jbuf, sems, live):
    def copy(i):
        part = pl.ds(i * CHUNK, CHUNK)
        return pltpu.make_async_copy(jac.at[part], jbuf.at[part], sems.at[i])

    groups = (live + GROUP - 1) // GROUP
    per = GROUP // CHUNK

    for i in range(jac.shape[0] // CHUNK):
        @pl.when(i < groups * per)
        def _():
            copy(i).start()

    def arrive(g):
        for i in range(per):
            copy(g * per + i).wait()

    return groups, arrive


def synth_from(state, bufs, model):
    src = None
    for level in reversed(range(LEVELS)):
        n = SEG_ROWS[level]
        base = SEG_OFF[level]
        if src is None:
            sm = state[SEG_OFF[5] + 4 : SEG_OFF[5] + 8 + n, :]
            sp = state[SEG_OFF[5] + 3 : SEG_OFF[5] + 7 + n, :]
        else:
            sm = src[4 : 8 + n, :]
            sp = src[3 : 7 + n, :]
        dm = state[base + 4 : base + 8 + n, :]
        dp = state[base + 3 : base + 7 + n, :]
        even = low_pass[0] * sm + high_pass[0] * dm + low_pass[2] * sp + high_pass[2] * dp
        odd = low_pass[1] * sm + high_pass[1] * dm + low_pass[3] * sp + high_pass[3] * dp
        dst = bufs[level]
        dst[pl.ds(0, n + 4, stride=2), :] = even
        dst[pl.ds(1, n + 4, stride=2), :] = odd
        src = dst
    model[...] = src[8:1032, :].astype(bf16)


SYNTH_BUFS = [pltpu.VMEM((8 + 2 * SEG_ROWS[l], 128), f32) for l in range(LEVELS)]


def early_kernel(state, model, *bufs):
    synth_from(state, bufs, model)


def synth_kernel(state_in, recv, state, fix, *scratch):
    state[...] = state_in[...]
    for g in range(6):
        base = SEG_OFF[g]
        own = state_in[base : base + 8, :]
        got = pltpu.roll(recv[8 * g : 8 * g + 8, :], 32, 1)
        state[base : base + 8, :] = jnp.where(lanes((8, 128)) < 32, got, own)
    model = scratch[-1]
    synth_from(state, scratch[:-1], model)
    fix[...] = model[0:128, :]


def first_kernel(rows, cols, cnt, place, f0, f1, f2, f3, *refs):
    fwd_kernel(rows, cols, cnt, place, *refs, fixes=(f0, f1, f2, f3))


def fwd_kernel(
    rows, cols, cnt, place, p0, p1, p2, p3, jac, keep, send, jbuf, model, acc, sems, fixes=None
):
    live = cnt[0]
    core = place[2]
    groups, arrive = tile_copies(jac, jbuf, sems, live)
    acc[...] = jnp.zeros(acc.shape, f32)
    for c in range(CELL_TILES):
        q, t = c // 8, c % 8
        pieces = fixes if c == 0 and fixes else (p0, p1, p2, p3)
        model[c] = jnp.concatenate(
            [p[128 * t : 128 * t + 128, 32 * q : 32 * q + 32] for p in pieces], axis=1
        )

    def group(g, carry):
        arrive(g)
        for v in range(GROUP):
            s = g * GROUP + v
            r = jnp.where(s < live, rows[s], ROW_BLOCKS)
            acc[r] += jnp.dot(jbuf[s], model[cols[s]], preferred_element_type=f32)
        return carry

    lax.fori_loop(0, groups, group, 0)
    for xz in range(16):
        for h in range(2):
            keep[2 * xz + h] = acc[4 * xz + 2 * core + h]
            send[2 * xz + h] = acc[4 * xz + 2 * (1 - core) + h].astype(bf16)


def split_kernel(place, keep, recv, own, s1, s2, s3):
    first, _, step, other = axes(place, place[2])
    for k, out in enumerate((own, s1, s2, s3)):
        for e in range(4):
            for h in range(2):
                b = 2 * (step * ((first + k) % 4) + other * e) + h
                out[2 * e + h] = (keep[b] + recv[b].astype(f32)).astype(out.dtype)


def gather_kernel(own, r1, r2, r3, total, sent):
    for i in range(8):
        s = own[i] + r1[i].astype(f32) + r2[i].astype(f32) + r3[i].astype(f32)
        total[i] = s
        sent[i] = s.astype(bf16)


def misfit_tile(own, r1, r2, r3, obs, i):
    return own[i] + r1[i].astype(f32) + r2[i].astype(f32) + r3[i].astype(f32) - obs[i]


def obs_kernel(place, obs, out):
    back = (128 - 32 * place[3]) % 128
    for i in range(8):
        out[i] = pltpu.roll(obs[i // 2, 128 * (i % 2) : 128 * (i % 2) + 128, :], back, 1)


def misfit_kernel(own, r1, r2, r3, obs, rounded):
    for i in range(8):
        rounded[i] = misfit_tile(own, r1, r2, r3, obs, i).T.astype(bf16)


def share_kernel(place, own, r1, r2, r3, obs, share):
    for h in range(2):
        tile = misfit_tile(own, r1, r2, r3, obs, 2 * axes(place, place[2])[1] + h)
        share[128 * h : 128 * h + 128, :] = pltpu.roll(tile, 32 * place[3], 1)


def bwd_kernel(rows, cols, cnt, place, *refs):
    jac, g0, g1, g2, g3, e0, e1, e2, e3, jbuf, mis, acc, sems = refs[8:]
    live = cnt[0]
    core = place[2]
    groups, arrive = tile_copies(jac, jbuf, sems, live)
    acc[...] = jnp.zeros(acc.shape, f32)
    for pieces, c in ((refs[0:4], core), (refs[4:8], 1 - core)):
        first, _, step, other = axes(place, c)
        for k in range(4):
            b = 4 * step * ((first + k) % 4) + 2 * c
            for e in range(4):
                for h in range(2):
                    mis[b + 4 * other * e + h] = pieces[k][2 * e + h]

    def group(g, carry):
        arrive(g)
        for v in range(GROUP):
            s = g * GROUP + v
            c = jnp.where(s < live, cols[s], CELL_TILES)
            acc[c] += jnp.dot(mis[rows[s]], jbuf[s], preferred_element_type=f32)
        return carry

    lax.fori_loop(0, groups, group, 0)
    for k, out in enumerate((e0, e1, e2, e3)):
        part = slice(32 * k, 32 * k + 32)
        edge = jnp.where(lanes((32, 128)) < 64, acc[0, part, :], acc[CELL_TILES - 1, part, :])
        out[...] = edge.astype(out.dtype)
    for k, out in enumerate((g0, g1, g2, g3)):
        for t in range(8):
            for q in range(4):
                out[t, 32 * q : 32 * q + 32, :] = acc[8 * q + t, 32 * k : 32 * k + 32, :].astype(out.dtype)


def edge_kernel(own, r1, r2, r3, edge):
    edge[...] = own[...] + r1[...].astype(f32) + r2[...].astype(f32) + r3[...].astype(f32)


def wave_update(own, r1, r2, r3, nxt, prv, state_in, state, ext, levels):
    for i in range(8):
        s = own[i] + r1[i].astype(f32) + r2[i].astype(f32) + r3[i].astype(f32)
        ext[64 + 128 * i : 192 + 128 * i, :] = s.T
    ln = lanes((64, 128))
    near = jnp.concatenate([prv[...], jnp.zeros((64, 128), f32), nxt[...]], axis=0).T
    ext[0:64, :] = jnp.where(ln < 32, near[64:, :], pltpu.roll(ext[1024:1088, :], 32, 1))
    ext[1088:1152, :] = jnp.where(ln >= 96, near[:64, :], pltpu.roll(ext[64:128, :], 96, 1))
    ext[1152:1160, :] = jnp.zeros((8, 128), f32)
    src = ext
    for level in range(LEVELS):
        count = [576, 288, 144, 72, 40][level]
        front = 64 >> (level + 1)
        n = SEG_ROWS[level]
        base = SEG_OFF[level]
        e0 = src[pl.ds(0, count, stride=2), :]
        o0 = src[pl.ds(1, count, stride=2), :]
        e1 = src[pl.ds(2, count, stride=2), :]
        o1 = src[pl.ds(3, count, stride=2), :]
        smooth = low_pass[0] * e0 + low_pass[1] * o0 + low_pass[2] * e1 + low_pass[3] * o1
        detail = high_pass[0] * e0 + high_pass[1] * o0 + high_pass[2] * e1 + high_pass[3] * o1
        lead = min(front, 8)
        part = detail[front - lead : front + n, :]
        moved = state_in[base + 8 - lead : base + 8 + n, :] - step_length * part
        state[base + 8 - lead : base + 8 + n, :] = moved - jnp.clip(moved, -threshold, threshold)
        if lead < 8:
            state[base : base + 8 - lead, :] = jnp.zeros((8 - lead, 128), f32)
        if level < LEVELS - 1:
            dst = levels[level]
            dst[0:count, :] = smooth
            dst[count:, :] = jnp.zeros((dst.shape[0] - count, 128), f32)
            src = dst
        else:
            base = SEG_OFF[5]
            part = smooth[front - lead : front + n, :]
            state[base + 8 - lead : base + 8 + n, :] = (
                state_in[base + 8 - lead : base + 8 + n, :] - step_length * part
            )
            state[base : base + 8 - lead, :] = jnp.zeros((8 - lead, 128), f32)


WAVE_BUFS = [pltpu.VMEM((1160, 128), f32)] + [
    pltpu.VMEM((rows, 128), f32) for rows in (584, 296, 152, 88)
]


def wave_kernel(
    own, r1, r2, r3, nxt, prv, state_in, state, model, ext, l0, l1, l2, l3, *bufs
):
    wave_update(own, r1, r2, r3, nxt, prv, state_in, state, ext, (l0, l1, l2, l3))
    synth_from(state, bufs, model)


def last_kernel(own, r1, r2, r3, nxt, prv, state_in, out, state, ext, l0, l1, l2, l3):
    wave_update(own, r1, r2, r3, nxt, prv, state_in, state, ext, (l0, l1, l2, l3))
    for g in range(6):
        n = SEG_ROWS[g]
        base = SEG_OFF[g]
        tile = state[base + 8 : base + 8 + n, :].T
        for q in range(4):
            out[:, COEF_OFF[g] + q * n : COEF_OFF[g] + (q + 1) * n] = tile[32 * q : 32 * q + 32, :]


def from_ahead(x, axis, by):
    n = lax.axis_size(axis)
    return lax.ppermute(x, axis, [(i, (i - by) % n) for i in range(n)])


def to_ahead(x, axis, by):
    n = lax.axis_size(axis)
    return lax.ppermute(x, axis, [(i, (i + by) % n) for i in range(n)])


def by_core(x, stage, by):
    pairs = []
    for i in range(4):
        for j in range(4):
            for c in range(2):
                to = (i, (j + by) % 4) if c == stage else ((i + by) % 4, j)
                pairs.append((8 * i + 2 * j + c, 8 * to[0] + 2 * to[1] + c))
    return lax.ppermute(x, MP, pairs)


MP = ("x", "z", "core")


def three(xs, move):
    out = []
    for k in (1, 2, 3):
        out.append(move(xs[k - 1], k))
    return out


def along(x, by):
    return lax.ppermute(x, MP, [(i, (i + by) % 32) for i in range(32)])


def body(coeffs_start, observed, jacobian_tiles, tile_rows, tile_cols, tile_count):
    jac = jacobian_tiles[0, 0]
    rows = tile_rows[0, 0]
    cols = tile_cols[0, 0]
    cnt = tile_count[0]
    n_slots = jac.shape[0]
    x, z, core, ray = (lax.axis_index(a) for a in ("x", "z", "core", "ray"))
    place = jnp.stack([x, z, core, ray]).astype(jnp.int32)
    tiles = sds((8, 128, 128), f32)
    tiles_b = sds((8, 128, 128), bf16)
    flat_b = sds((1024, 128), bf16)

    state, tails = call(
        init_kernel, [VM], [sds((STATE_ROWS, 128), f32), sds((48, 128), f32)]
    )(coeffs_start.T)
    obs_all = observed.reshape(4, 4, 2, 256, 128)
    obs_rows = lax.cond(
        core == 0,
        lambda a: lax.dynamic_slice(a, (0, z, 0, 0, 0), (4, 1, 1, 256, 128)).reshape(4, 256, 128),
        lambda a: lax.dynamic_slice(a, (x, 0, 1, 0, 0), (1, 4, 1, 256, 128)).reshape(4, 256, 128),
        obs_all,
    )
    (obs_t,) = call(obs_kernel, [SM, VM], [tiles])(place, obs_rows)
    recv = along(tails, 1)
    (model,) = call(early_kernel, [VM], [flat_b], SYNTH_BUFS)(state)
    state, fix = call(
        synth_kernel,
        [VM, VM],
        [sds((STATE_ROWS, 128), f32), sds((128, 128), bf16)],
        SYNTH_BUFS + [pltpu.VMEM((1024, 128), bf16)],
    )(state, recv)

    jac_scratch = pltpu.VMEM((n_slots, TILE, TILE), bf16)
    sems = pltpu.SemaphoreType.DMA((n_slots // CHUNK,))
    for sweep in range(ITERS):
        pull = lambda a, k: from_ahead(a, "ray", k)
        push = lambda a, k: to_ahead(a, "ray", k)
        pieces = [model] + three([model] * 3, pull)
        fixes = []
        if sweep == 0:
            fixes = [fix] + three([fix] * 3, pull)
        keep, send = call(
            fwd_kernel if sweep else first_kernel,
            [SM] * 4 + [VM] * (4 + len(fixes)) + [ANY],
            [sds((32, 128, 128), f32), sds((32, 128, 128), bf16)],
            [jac_scratch, pltpu.VMEM((32, 128, 128), bf16), pltpu.VMEM((65, 128, 128), f32), sems],
        )(rows, cols, cnt, place, *fixes, *pieces, jac)
        got = to_ahead(send, "core", 1)
        own, s1, s2, s3 = call(
            split_kernel, [SM, VM, VM], [tiles, tiles_b, tiles_b, tiles_b]
        )(place, keep, got)
        r = three((s1, s2, s3), lambda a, k: by_core(a, 0, k))
        own, sent = call(gather_kernel, [VM] * 4, [tiles, tiles_b])(own, *r)
        r = three([sent] * 3, lambda a, k: by_core(a, 1, k))
        (rounded,) = call(misfit_kernel, [VM] * 5, [tiles_b])(own, *r, obs_t)
        if sweep == ITERS - 1:
            (share,) = call(share_kernel, [SM] + [VM] * 5, [sds((256, 128), f32)])(
                place, own, *r, obs_t
            )
        mine = [rounded] + three([rounded] * 3, lambda a, k: by_core(a, 0, -k))
        other = [to_ahead(m, "core", 1) for m in mine]
        edge, edge_b = sds((32, 128), f32), sds((32, 128), bf16)
        g0, g1, g2, g3, e0, e1, e2, e3 = call(
            bwd_kernel,
            [SM, SM, SM, SM] + [VM] * 8 + [ANY],
            [tiles, tiles_b, tiles_b, tiles_b, edge, edge_b, edge_b, edge_b],
            [jac_scratch, pltpu.VMEM((64, 128, 128), bf16), pltpu.VMEM((33, 128, 128), f32), sems],
        )(rows, cols, cnt, place, *mine, *other, jac)
        r = three((e1, e2, e3), push)
        (near,) = call(edge_kernel, [VM] * 4, [edge])(e0, *r)
        nxt = along(near, -1)
        prv = along(near, 1) if sweep < ITERS - 1 else near
        r = three((g1, g2, g3), push)
        if sweep < ITERS - 1:
            state, model = call(
                wave_kernel, [VM] * 7, [sds((STATE_ROWS, 128), f32), flat_b], WAVE_BUFS + SYNTH_BUFS
            )(g0, *r, nxt, prv, state)
        else:
            (coeffs,) = call(
                last_kernel,
                [VM] * 7,
                [sds((32, 4096), f32)],
                [pltpu.VMEM((STATE_ROWS, 128), f32)] + WAVE_BUFS,
            )(g0, *r, nxt, prv, state)
    return (coeffs.T, share)


def solution(mesh):
    fine = Mesh(mesh.devices.reshape(4, 4, 4, 2), ("ray", "x", "z", "core"))
    placed = (
        P(MP, "ray"),
        P("ray", None),
        P("ray", MP, None, None, None),
        P("ray", MP, None),
        P("ray", MP, None),
        P("ray", MP),
    )
    return jax.shard_map(
        body,
        mesh=fine,
        in_specs=placed,
        out_specs=(P(MP, "ray"), P(("ray",) + MP, None)),
        check_vma=False,
    )
```

```python
import math

import jax
import jax.numpy as jnp
from jax import lax
from jax.experimental import pallas as pl
from jax.experimental.pallas import tpu as pltpu
from jax.sharding import Mesh, PartitionSpec as P


LEVELS = 5
ITERS = 2
TILE = 128
GROUP = 48
CHUNK = 16
ROW_BLOCKS = 64
CELL_TILES = 32


root_three = math.sqrt(3.0)
norm_factor = 4.0 * math.sqrt(2.0)
low_pass = [
    (1.0 + root_three) / norm_factor,
    (3.0 + root_three) / norm_factor,
    (3.0 - root_three) / norm_factor,
    (1.0 - root_three) / norm_factor,
]
high_pass = [low_pass[3], -low_pass[2], low_pass[1], -low_pass[0]]
step_length = 0.5
threshold = 0.1

f32 = jnp.float32
bf16 = jnp.bfloat16

SEG_ROWS = [512, 256, 128, 64, 32, 32]
SEG_OFF = [0]
for n in SEG_ROWS:
    SEG_OFF.append(SEG_OFF[-1] + 8 + n)
STATE_ROWS = SEG_OFF[-1]
COEF_OFF = [0, 2048, 3072, 3584, 3840, 3968]

VM = pl.BlockSpec(memory_space=pltpu.VMEM)
SM = pl.BlockSpec(memory_space=pltpu.SMEM)
ANY = pl.BlockSpec(memory_space=pl.ANY)


def sds(shape, dtype):
    return jax.ShapeDtypeStruct(shape, dtype)


def call(kernel, in_specs, outs, scratch=(), mib=40):
    return pl.pallas_call(
        kernel,
        in_specs=in_specs,
        out_specs=[VM] * len(outs),
        out_shape=outs,
        scratch_shapes=list(scratch),
        compiler_params=pltpu.CompilerParams(vmem_limit_bytes=mib * 1024 * 1024),
    )


def lanes(shape):
    return lax.broadcasted_iota(jnp.int32, shape, 1)


def init_kernel(coeffs, state, tails):
    for g in range(6):
        n = SEG_ROWS[g]
        base = SEG_OFF[g]
        parts = [coeffs[:, COEF_OFF[g] + q * n : COEF_OFF[g] + (q + 1) * n] for q in range(4)]
        packed = jnp.concatenate(parts, axis=0).T
        state[base + 8 : base + 8 + n, :] = packed
        last = packed[n - 8 : n, :]
        state[base : base + 8, :] = pltpu.roll(last, 32, 1)
        tails[8 * g : 8 * g + 8, :] = last


def axes(place, core):
    first = jnp.where(core == 0, place[1], place[0])
    second = jnp.where(core == 0, place[0], place[1])
    step = jnp.where(core == 0, 1, 4)
    return first, second, step, 5 - step


def tile_copies(jac, jbuf, sems, live):
    def copy(i):
        part = pl.ds(i * CHUNK, CHUNK)
        return pltpu.make_async_copy(jac.at[part], jbuf.at[part], sems.at[i])

    groups = (live + GROUP - 1) // GROUP
    per = GROUP // CHUNK

    for i in range(jac.shape[0] // CHUNK):
        @pl.when(i < groups * per)
        def _():
            copy(i).start()

    def arrive(g):
        for i in range(per):
            copy(g * per + i).wait()

    return groups, arrive


def synth_from(state, bufs, model):
    src = None
    for level in reversed(range(LEVELS)):
        n = SEG_ROWS[level]
        base = SEG_OFF[level]
        if src is None:
            sm = state[SEG_OFF[5] + 4 : SEG_OFF[5] + 8 + n, :]
            sp = state[SEG_OFF[5] + 3 : SEG_OFF[5] + 7 + n, :]
        else:
            sm = src[4 : 8 + n, :]
            sp = src[3 : 7 + n, :]
        dm = state[base + 4 : base + 8 + n, :]
        dp = state[base + 3 : base + 7 + n, :]
        even = low_pass[0] * sm + high_pass[0] * dm + low_pass[2] * sp + high_pass[2] * dp
        odd = low_pass[1] * sm + high_pass[1] * dm + low_pass[3] * sp + high_pass[3] * dp
        dst = bufs[level]
        dst[pl.ds(0, n + 4, stride=2), :] = even
        dst[pl.ds(1, n + 4, stride=2), :] = odd
        src = dst
    model[...] = src[8:1032, :].astype(bf16)


SYNTH_BUFS = [pltpu.VMEM((8 + 2 * SEG_ROWS[l], 128), f32) for l in range(LEVELS)]


def early_kernel(state, model, *bufs):
    synth_from(state, bufs, model)


def synth_kernel(state_in, recv, state, fix, *scratch):
    state[...] = state_in[...]
    for g in range(6):
        base = SEG_OFF[g]
        own = state_in[base : base + 8, :]
        got = pltpu.roll(recv[8 * g : 8 * g + 8, :], 32, 1)
        state[base : base + 8, :] = jnp.where(lanes((8, 128)) < 32, got, own)
    model = scratch[-1]
    synth_from(state, scratch[:-1], model)
    fix[...] = model[0:128, :]


def first_kernel(rows, cols, cnt, place, f0, f1, f2, f3, *refs):
    fwd_kernel(rows, cols, cnt, place, *refs, fixes=(f0, f1, f2, f3))


def fwd_kernel(
    rows, cols, cnt, place, p0, p1, p2, p3, jac, acc, t0, t1, t2, t3, jbuf, model, sems, fixes=None
):
    groups, arrive = tile_copies(jac, jbuf, sems, cnt[0])
    acc[...] = jnp.zeros(acc.shape, f32)
    for c in range(CELL_TILES):
        q, t = c // 8, c % 8
        pieces = fixes if c == 0 and fixes else (p0, p1, p2, p3)
        model[c] = jnp.concatenate(
            [p[128 * t : 128 * t + 128, 32 * q : 32 * q + 32] for p in pieces], axis=1
        )

    def group(g, carry):
        arrive(g)
        for v in range(GROUP):
            s = g * GROUP + v
            acc[rows[s]] += jnp.dot(jbuf[s], model[cols[s]], preferred_element_type=f32)
        return carry

    lax.fori_loop(0, groups, group, 0)
    first, _, step, other = axes(place, 1 - place[2])
    for k, out in enumerate((t0, t1, t2, t3)):
        for e in range(4):
            for h in range(2):
                b = ROW_BLOCKS // 2 + 2 * (step * ((first + k) % 4) + other * e) + h
                out[2 * e + h] = acc[b].astype(bf16)


def split_kernel(k):
    def kernel(place, acc, recv, out):
        first, _, step, other = axes(place, place[2])
        for e in range(4):
            for h in range(2):
                b = 2 * (step * ((first + k) % 4) + other * e) + h
                out[2 * e + h] = (acc[b] + recv[2 * e + h].astype(f32)).astype(out.dtype)

    return kernel


def gather_kernel(own, r1, r2, r3, total, sent):
    for i in range(8):
        s = own[i] + r1[i].astype(f32) + r2[i].astype(f32) + r3[i].astype(f32)
        total[i] = s
        sent[i] = s.astype(bf16)


def misfit_tile(own, r1, r2, r3, obs, i):
    return own[i] + r1[i].astype(f32) + r2[i].astype(f32) + r3[i].astype(f32) - obs[i]


def obs_kernel(place, obs, out):
    back = (128 - 32 * place[3]) % 128
    for i in range(8):
        out[i] = pltpu.roll(obs[i // 2, 128 * (i % 2) : 128 * (i % 2) + 128, :], back, 1)


def misfit_kernel(own, r1, r2, r3, obs, rounded):
    for i in range(8):
        rounded[i] = misfit_tile(own, r1, r2, r3, obs, i).T.astype(bf16)


def share_kernel(place, own, r1, r2, r3, obs, share):
    for h in range(2):
        tile = misfit_tile(own, r1, r2, r3, obs, 2 * axes(place, place[2])[1] + h)
        share[128 * h : 128 * h + 128, :] = pltpu.roll(tile, 32 * place[3], 1)


def bwd_kernel(rows, cols, cnt, place, *refs):
    jac, g0, g1, g2, g3, e0, e1, e2, e3, jbuf, mis, acc, sems = refs[8:]
    live = cnt[0]
    core = place[2]
    groups, arrive = tile_copies(jac, jbuf, sems, live)
    acc[...] = jnp.zeros(acc.shape, f32)
    for pieces, c in ((refs[0:4], core), (refs[4:8], 1 - core)):
        first, _, step, other = axes(place, c)
        for k in range(4):
            b = 4 * step * ((first + k) % 4) + 2 * c
            for e in range(4):
                for h in range(2):
                    mis[b + 4 * other * e + h] = pieces[k][2 * e + h]

    def group(g, carry):
        arrive(g)
        for v in range(GROUP):
            s = g * GROUP + v
            acc[cols[s]] += jnp.dot(mis[rows[s]], jbuf[s], preferred_element_type=f32)
        return carry

    lax.fori_loop(0, groups, group, 0)
    for k, out in enumerate((e0, e1, e2, e3)):
        part = slice(32 * k, 32 * k + 32)
        edge = jnp.where(lanes((32, 128)) < 64, acc[0, part, :], acc[CELL_TILES - 1, part, :])
        out[...] = edge.astype(out.dtype)
    for k, out in enumerate((g0, g1, g2, g3)):
        for t in range(8):
            for q in range(4):
                out[t, 32 * q : 32 * q + 32, :] = acc[8 * q + t, 32 * k : 32 * k + 32, :].astype(out.dtype)


def edge_kernel(own, r1, r2, r3, edge):
    edge[...] = own[...] + r1[...].astype(f32) + r2[...].astype(f32) + r3[...].astype(f32)


def wave_update(own, r1, r2, r3, nxt, prv, state_in, state, ext, levels):
    for i in range(8):
        s = own[i] + r1[i].astype(f32) + r2[i].astype(f32) + r3[i].astype(f32)
        ext[64 + 128 * i : 192 + 128 * i, :] = s.T
    ln = lanes((64, 128))
    near = jnp.concatenate([prv[...], jnp.zeros((64, 128), f32), nxt[...]], axis=0).T
    ext[0:64, :] = jnp.where(ln < 32, near[64:, :], pltpu.roll(ext[1024:1088, :], 32, 1))
    ext[1088:1152, :] = jnp.where(ln >= 96, near[:64, :], pltpu.roll(ext[64:128, :], 96, 1))
    ext[1152:1160, :] = jnp.zeros((8, 128), f32)
    src = ext
    for level in range(LEVELS):
        count = [576, 288, 144, 72, 40][level]
        front = 64 >> (level + 1)
        n = SEG_ROWS[level]
        base = SEG_OFF[level]
        e0 = src[pl.ds(0, count, stride=2), :]
        o0 = src[pl.ds(1, count, stride=2), :]
        e1 = src[pl.ds(2, count, stride=2), :]
        o1 = src[pl.ds(3, count, stride=2), :]
        smooth = low_pass[0] * e0 + low_pass[1] * o0 + low_pass[2] * e1 + low_pass[3] * o1
        detail = high_pass[0] * e0 + high_pass[1] * o0 + high_pass[2] * e1 + high_pass[3] * o1
        lead = min(front, 8)
        part = detail[front - lead : front + n, :]
        moved = state_in[base + 8 - lead : base + 8 + n, :] - step_length * part
        state[base + 8 - lead : base + 8 + n, :] = moved - jnp.clip(moved, -threshold, threshold)
        if lead < 8:
            state[base : base + 8 - lead, :] = jnp.zeros((8 - lead, 128), f32)
        if level < LEVELS - 1:
            dst = levels[level]
            dst[0:count, :] = smooth
            dst[count:, :] = jnp.zeros((dst.shape[0] - count, 128), f32)
            src = dst
        else:
            base = SEG_OFF[5]
            part = smooth[front - lead : front + n, :]
            state[base + 8 - lead : base + 8 + n, :] = (
                state_in[base + 8 - lead : base + 8 + n, :] - step_length * part
            )
            state[base : base + 8 - lead, :] = jnp.zeros((8 - lead, 128), f32)


WAVE_BUFS = [pltpu.VMEM((1160, 128), f32)] + [
    pltpu.VMEM((rows, 128), f32) for rows in (584, 296, 152, 88)
]


def wave_kernel(
    own, r1, r2, r3, nxt, prv, state_in, state, model, ext, l0, l1, l2, l3, *bufs
):
    wave_update(own, r1, r2, r3, nxt, prv, state_in, state, ext, (l0, l1, l2, l3))
    synth_from(state, bufs, model)


def last_kernel(own, r1, r2, r3, nxt, prv, state_in, out, state, ext, l0, l1, l2, l3):
    wave_update(own, r1, r2, r3, nxt, prv, state_in, state, ext, (l0, l1, l2, l3))
    for g in range(6):
        n = SEG_ROWS[g]
        base = SEG_OFF[g]
        tile = state[base + 8 : base + 8 + n, :].T
        for q in range(4):
            out[:, COEF_OFF[g] + q * n : COEF_OFF[g] + (q + 1) * n] = tile[32 * q : 32 * q + 32, :]


def from_ahead(x, axis, by):
    n = lax.axis_size(axis)
    return lax.ppermute(x, axis, [(i, (i - by) % n) for i in range(n)])


def to_ahead(x, axis, by):
    n = lax.axis_size(axis)
    return lax.ppermute(x, axis, [(i, (i + by) % n) for i in range(n)])


def by_core(x, stage, by):
    pairs = []
    for i in range(4):
        for j in range(4):
            for c in range(2):
                to = (i, (j + by) % 4) if c == stage else ((i + by) % 4, j)
                pairs.append((8 * i + 2 * j + c, 8 * to[0] + 2 * to[1] + c))
    return lax.ppermute(x, MP, pairs)


MP = ("x", "z", "core")


def three(xs, move):
    out = []
    for k in (1, 2, 3):
        out.append(move(xs[k - 1], k))
    return out


def along(x, by):
    return lax.ppermute(x, MP, [(i, (i + by) % 32) for i in range(32)])


def body(coeffs_start, observed, jacobian_tiles, tile_rows, tile_cols, tile_count):
    jac = jacobian_tiles[0, 0]
    rows = tile_rows[0, 0]
    cols = tile_cols[0, 0]
    cnt = tile_count[0]
    n_slots = jac.shape[0]
    live = jnp.arange(n_slots, dtype=jnp.int32) < cnt[0]
    x, z, core, ray = (lax.axis_index(a) for a in ("x", "z", "core", "ray"))
    place = jnp.stack([x, z, core, ray]).astype(jnp.int32)
    fwd_rows = rows // 4 * 2 + rows % 2 + ROW_BLOCKS // 2 * (rows // 2 % 2 != core)
    fwd_rows = jnp.where(live, fwd_rows, ROW_BLOCKS)
    bwd_cols = jnp.where(live, cols, CELL_TILES)
    tiles = sds((8, 128, 128), f32)
    tiles_b = sds((8, 128, 128), bf16)
    flat_b = sds((1024, 128), bf16)

    state, tails = call(
        init_kernel, [VM], [sds((STATE_ROWS, 128), f32), sds((48, 128), f32)]
    )(coeffs_start.T)
    obs_all = observed.reshape(4, 4, 2, 256, 128)
    obs_rows = lax.cond(
        core == 0,
        lambda a: lax.dynamic_slice(a, (0, z, 0, 0, 0), (4, 1, 1, 256, 128)).reshape(4, 256, 128),
        lambda a: lax.dynamic_slice(a, (x, 0, 1, 0, 0), (1, 4, 1, 256, 128)).reshape(4, 256, 128),
        obs_all,
    )
    (obs_t,) = call(obs_kernel, [SM, VM], [tiles])(place, obs_rows)
    recv = along(tails, 1)
    (model,) = call(early_kernel, [VM], [flat_b], SYNTH_BUFS)(state)
    state, fix = call(
        synth_kernel,
        [VM, VM],
        [sds((STATE_ROWS, 128), f32), sds((128, 128), bf16)],
        SYNTH_BUFS + [pltpu.VMEM((1024, 128), bf16)],
    )(state, recv)

    jac_scratch = pltpu.VMEM((n_slots, TILE, TILE), bf16)
    sems = pltpu.SemaphoreType.DMA((n_slots // CHUNK,))
    for sweep in range(ITERS):
        pull = lambda a, k: from_ahead(a, "ray", k)
        push = lambda a, k: to_ahead(a, "ray", k)
        pieces = [model] + three([model] * 3, pull)
        fixes = []
        if sweep == 0:
            fixes = [fix] + three([fix] * 3, pull)
        acc, *sends = call(
            fwd_kernel if sweep else first_kernel,
            [SM] * 4 + [VM] * (4 + len(fixes)) + [ANY],
            [sds((ROW_BLOCKS + 1, 128, 128), f32)] + [tiles_b] * 4,
            [jac_scratch, pltpu.VMEM((32, 128, 128), bf16), sems],
        )(fwd_rows, cols, cnt, place, *fixes, *pieces, jac)
        parts = [None] * 4
        for k in (2, 1, 3, 0):
            got = to_ahead(sends[k], "core", 1)
            (parts[k],) = call(
                split_kernel(k), [SM, VM, VM], [tiles_b if k else tiles]
            )(place, acc, got)
        own = parts[0]
        r = three(parts[1:], lambda a, k: by_core(a, 0, k))
        own, sent = call(gather_kernel, [VM] * 4, [tiles, tiles_b])(own, *r)
        r = three([sent] * 3, lambda a, k: by_core(a, 1, k))
        (rounded,) = call(misfit_kernel, [VM] * 5, [tiles_b])(own, *r, obs_t)
        if sweep == ITERS - 1:
            (share,) = call(share_kernel, [SM] + [VM] * 5, [sds((256, 128), f32)])(
                place, own, *r, obs_t
            )
        mine = [rounded] + three([rounded] * 3, lambda a, k: by_core(a, 0, -k))
        other = [to_ahead(m, "core", 1) for m in mine]
        edge, edge_b = sds((32, 128), f32), sds((32, 128), bf16)
        g0, g1, g2, g3, e0, e1, e2, e3 = call(
            bwd_kernel,
            [SM, SM, SM, SM] + [VM] * 8 + [ANY],
            [tiles, tiles_b, tiles_b, tiles_b, edge, edge_b, edge_b, edge_b],
            [jac_scratch, pltpu.VMEM((64, 128, 128), bf16), pltpu.VMEM((33, 128, 128), f32), sems],
        )(rows, bwd_cols, cnt, place, *mine, *other, jac)
        r = three((e1, e2, e3), push)
        (near,) = call(edge_kernel, [VM] * 4, [edge])(e0, *r)
        nxt = along(near, -1)
        prv = along(near, 1) if sweep < ITERS - 1 else near
        r = three((g1, g2, g3), push)
        if sweep < ITERS - 1:
            state, model = call(
                wave_kernel, [VM] * 7, [sds((STATE_ROWS, 128), f32), flat_b], WAVE_BUFS + SYNTH_BUFS
            )(g0, *r, nxt, prv, state)
        else:
            (coeffs,) = call(
                last_kernel,
                [VM] * 7,
                [sds((32, 4096), f32)],
                [pltpu.VMEM((STATE_ROWS, 128), f32)] + WAVE_BUFS,
            )(g0, *r, nxt, prv, state)
    return (coeffs.T, share)


def solution(mesh):
    fine = Mesh(mesh.devices.reshape(4, 4, 4, 2), ("ray", "x", "z", "core"))
    placed = (
        P(MP, "ray"),
        P("ray", None),
        P("ray", MP, None, None, None),
        P("ray", MP, None),
        P("ray", MP, None),
        P("ray", MP),
    )
    return jax.shard_map(
        body,
        mesh=fine,
        in_specs=placed,
        out_specs=(P(MP, "ray"), P(("ray",) + MP, None)),
        check_vma=False,
    )
```

```python
import math

import jax
import jax.numpy as jnp
from jax import lax
from jax.experimental import pallas as pl
from jax.experimental.pallas import tpu as pltpu
from jax.sharding import Mesh, PartitionSpec as P


LEVELS = 5
ITERS = 2
TILE = 128
GROUP = 64
CHUNK = 16
ROW_BLOCKS = 64
CELL_TILES = 32


root_three = math.sqrt(3.0)
norm_factor = 4.0 * math.sqrt(2.0)
low_pass = [
    (1.0 + root_three) / norm_factor,
    (3.0 + root_three) / norm_factor,
    (3.0 - root_three) / norm_factor,
    (1.0 - root_three) / norm_factor,
]
high_pass = [low_pass[3], -low_pass[2], low_pass[1], -low_pass[0]]
step_length = 0.5
threshold = 0.1

f32 = jnp.float32
bf16 = jnp.bfloat16

SEG_ROWS = [512, 256, 128, 64, 32, 32]
SEG_OFF = [0]
for n in SEG_ROWS:
    SEG_OFF.append(SEG_OFF[-1] + 8 + n)
STATE_ROWS = SEG_OFF[-1]
COEF_OFF = [0, 2048, 3072, 3584, 3840, 3968]

VM = pl.BlockSpec(memory_space=pltpu.VMEM)
SM = pl.BlockSpec(memory_space=pltpu.SMEM)
ANY = pl.BlockSpec(memory_space=pl.ANY)


def sds(shape, dtype):
    return jax.ShapeDtypeStruct(shape, dtype)


def call(kernel, in_specs, outs, scratch=(), mib=40):
    return pl.pallas_call(
        kernel,
        in_specs=in_specs,
        out_specs=[VM] * len(outs),
        out_shape=outs,
        scratch_shapes=list(scratch),
        compiler_params=pltpu.CompilerParams(vmem_limit_bytes=mib * 1024 * 1024),
    )


def lanes(shape):
    return lax.broadcasted_iota(jnp.int32, shape, 1)


def init_kernel(coeffs, state, tails):
    for g in range(6):
        n = SEG_ROWS[g]
        base = SEG_OFF[g]
        parts = [coeffs[:, COEF_OFF[g] + q * n : COEF_OFF[g] + (q + 1) * n] for q in range(4)]
        packed = jnp.concatenate(parts, axis=0).T
        state[base + 8 : base + 8 + n, :] = packed
        last = packed[n - 8 : n, :]
        state[base : base + 8, :] = pltpu.roll(last, 32, 1)
        tails[8 * g : 8 * g + 8, :] = last


def axes(core):
    x, z = lax.axis_index("x"), lax.axis_index("z")
    first = jnp.where(core == 0, z, x)
    second = jnp.where(core == 0, x, z)
    step = jnp.where(core == 0, 1, 4)
    return first, second, step, 5 - step


def tile_copies(jac, jbuf, sems, live):
    def copy(i):
        part = pl.ds(i * CHUNK, CHUNK)
        return pltpu.make_async_copy(jac.at[part], jbuf.at[part], sems.at[i])

    groups = (live + GROUP - 1) // GROUP
    per = GROUP // CHUNK

    for i in range(jac.shape[0] // CHUNK):
        @pl.when(i < groups * per)
        def _():
            copy(i).start()

    def arrive(g):
        for i in range(per):
            copy(g * per + i).wait()

    return groups, arrive


def synth_from(state, bufs, model):
    src = None
    for level in reversed(range(LEVELS)):
        n = SEG_ROWS[level]
        base = SEG_OFF[level]
        if src is None:
            sm = state[SEG_OFF[5] + 4 : SEG_OFF[5] + 8 + n, :]
            sp = state[SEG_OFF[5] + 3 : SEG_OFF[5] + 7 + n, :]
        else:
            sm = src[4 : 8 + n, :]
            sp = src[3 : 7 + n, :]
        dm = state[base + 4 : base + 8 + n, :]
        dp = state[base + 3 : base + 7 + n, :]
        even = low_pass[0] * sm + high_pass[0] * dm + low_pass[2] * sp + high_pass[2] * dp
        odd = low_pass[1] * sm + high_pass[1] * dm + low_pass[3] * sp + high_pass[3] * dp
        dst = bufs[level]
        dst[pl.ds(0, n + 4, stride=2), :] = even
        dst[pl.ds(1, n + 4, stride=2), :] = odd
        src = dst
    model[...] = src[8:1032, :].astype(bf16)


SYNTH_BUFS = [pltpu.VMEM((8 + 2 * SEG_ROWS[l], 128), f32) for l in range(LEVELS)]


def early_kernel(state, model, *bufs):
    synth_from(state, bufs, model)


def synth_kernel(state_in, recv, state, fix, *scratch):
    state[...] = state_in[...]
    for g in range(6):
        base = SEG_OFF[g]
        own = state_in[base : base + 8, :]
        got = pltpu.roll(recv[8 * g : 8 * g + 8, :], 32, 1)
        state[base : base + 8, :] = jnp.where(lanes((8, 128)) < 32, got, own)
    model = scratch[-1]
    synth_from(state, scratch[:-1], model)
    fix[...] = model[0:128, :]


def first_kernel(table, f0, f1, f2, f3, *refs):
    fwd_kernel(table, *refs, fixes=(f0, f1, f2, f3))


def fwd_kernel(
    table, p0, p1, p2, p3, jac, keep, send, jbuf, model, acc, sems, fixes=None
):
    slots = jac.shape[0]
    live = table[2 * slots]
    core = lax.axis_index("core")
    groups, arrive = tile_copies(jac, jbuf, sems, live)
    acc[...] = jnp.zeros(acc.shape, f32)
    for c in range(CELL_TILES):
        q, t = c // 8, c % 8
        pieces = fixes if c == 0 and fixes else (p0, p1, p2, p3)
        model[c] = jnp.concatenate(
            [p[128 * t : 128 * t + 128, 32 * q : 32 * q + 32] for p in pieces], axis=1
        )

    def group(g, carry):
        arrive(g)
        for v in range(GROUP):
            s = g * GROUP + v
            r = jnp.where(s < live, table[s], ROW_BLOCKS)
            acc[r] += jnp.dot(jbuf[s], model[table[slots + s]], preferred_element_type=f32)
        return carry

    lax.fori_loop(0, groups, group, 0)
    for xz in range(16):
        for h in range(2):
            keep[2 * xz + h] = acc[4 * xz + 2 * core + h]
            send[2 * xz + h] = acc[4 * xz + 2 * (1 - core) + h].astype(bf16)


def split_kernel(keep, recv, own, s1, s2, s3):
    first, _, step, other = axes(lax.axis_index("core"))
    for k, out in enumerate((own, s1, s2, s3)):
        for e in range(4):
            for h in range(2):
                b = 2 * (step * ((first + k) % 4) + other * e) + h
                out[2 * e + h] = (keep[b] + recv[b].astype(f32)).astype(out.dtype)


def gather_kernel(own, r1, r2, r3, total, sent):
    for i in range(8):
        s = own[i] + r1[i].astype(f32) + r2[i].astype(f32) + r3[i].astype(f32)
        total[i] = s
        sent[i] = s.astype(bf16)


def misfit_tile(own, r1, r2, r3, obs, i):
    return own[i] + r1[i].astype(f32) + r2[i].astype(f32) + r3[i].astype(f32) - obs[i]


def obs_kernel(obs, out):
    back = (128 - 32 * lax.axis_index("ray")) % 128
    for i in range(8):
        out[i] = pltpu.roll(obs[i // 2, 128 * (i % 2) : 128 * (i % 2) + 128, :], back, 1)


def misfit_kernel(own, r1, r2, r3, obs, rounded):
    for i in range(8):
        rounded[i] = misfit_tile(own, r1, r2, r3, obs, i).T.astype(bf16)


def share_kernel(own, r1, r2, r3, obs, share):
    for h in range(2):
        tile = misfit_tile(own, r1, r2, r3, obs, 2 * axes(lax.axis_index("core"))[1] + h)
        share[128 * h : 128 * h + 128, :] = pltpu.roll(tile, 32 * lax.axis_index("ray"), 1)


def bwd_kernel(table, *refs):
    jac, g0, g1, g2, g3, e0, e1, e2, e3, jbuf, mis, acc, sems = refs[8:]
    slots = jac.shape[0]
    live = table[2 * slots]
    core = lax.axis_index("core")
    groups, arrive = tile_copies(jac, jbuf, sems, live)
    acc[...] = jnp.zeros(acc.shape, f32)
    for pieces, c in ((refs[0:4], core), (refs[4:8], 1 - core)):
        first, _, step, other = axes(c)
        for k in range(4):
            b = 4 * step * ((first + k) % 4) + 2 * c
            for e in range(4):
                for h in range(2):
                    mis[b + 4 * other * e + h] = pieces[k][2 * e + h]

    def group(g, carry):
        arrive(g)
        for v in range(GROUP):
            s = g * GROUP + v
            c = jnp.where(s < live, table[slots + s], CELL_TILES)
            acc[c] += jnp.dot(mis[table[s]], jbuf[s], preferred_element_type=f32)
        return carry

    lax.fori_loop(0, groups, group, 0)
    for k, out in enumerate((e0, e1, e2, e3)):
        part = slice(32 * k, 32 * k + 32)
        edge = jnp.where(lanes((32, 128)) < 64, acc[0, part, :], acc[CELL_TILES - 1, part, :])
        out[...] = edge.astype(out.dtype)
    for k, out in enumerate((g0, g1, g2, g3)):
        for t in range(8):
            for q in range(4):
                out[t, 32 * q : 32 * q + 32, :] = acc[8 * q + t, 32 * k : 32 * k + 32, :].astype(out.dtype)


def edge_kernel(own, r1, r2, r3, edge):
    edge[...] = own[...] + r1[...].astype(f32) + r2[...].astype(f32) + r3[...].astype(f32)


def wave_update(own, r1, r2, r3, nxt, prv, state_in, state, ext, levels):
    for i in range(8):
        s = own[i] + r1[i].astype(f32) + r2[i].astype(f32) + r3[i].astype(f32)
        ext[64 + 128 * i : 192 + 128 * i, :] = s.T
    ln = lanes((64, 128))
    near = jnp.concatenate([prv[...], jnp.zeros((64, 128), f32), nxt[...]], axis=0).T
    ext[0:64, :] = jnp.where(ln < 32, near[64:, :], pltpu.roll(ext[1024:1088, :], 32, 1))
    ext[1088:1152, :] = jnp.where(ln >= 96, near[:64, :], pltpu.roll(ext[64:128, :], 96, 1))
    ext[1152:1160, :] = jnp.zeros((8, 128), f32)
    src = ext
    for level in range(LEVELS):
        count = [576, 288, 144, 72, 40][level]
        front = 64 >> (level + 1)
        n = SEG_ROWS[level]
        base = SEG_OFF[level]
        e0 = src[pl.ds(0, count, stride=2), :]
        o0 = src[pl.ds(1, count, stride=2), :]
        e1 = src[pl.ds(2, count, stride=2), :]
        o1 = src[pl.ds(3, count, stride=2), :]
        smooth = low_pass[0] * e0 + low_pass[1] * o0 + low_pass[2] * e1 + low_pass[3] * o1
        detail = high_pass[0] * e0 + high_pass[1] * o0 + high_pass[2] * e1 + high_pass[3] * o1
        lead = min(front, 8)
        part = detail[front - lead : front + n, :]
        moved = state_in[base + 8 - lead : base + 8 + n, :] - step_length * part
        state[base + 8 - lead : base + 8 + n, :] = moved - jnp.clip(moved, -threshold, threshold)
        if lead < 8:
            state[base : base + 8 - lead, :] = jnp.zeros((8 - lead, 128), f32)
        if level < LEVELS - 1:
            dst = levels[level]
            dst[0:count, :] = smooth
            dst[count:, :] = jnp.zeros((dst.shape[0] - count, 128), f32)
            src = dst
        else:
            base = SEG_OFF[5]
            part = smooth[front - lead : front + n, :]
            state[base + 8 - lead : base + 8 + n, :] = (
                state_in[base + 8 - lead : base + 8 + n, :] - step_length * part
            )
            state[base : base + 8 - lead, :] = jnp.zeros((8 - lead, 128), f32)


WAVE_BUFS = [pltpu.VMEM((1160, 128), f32)] + [
    pltpu.VMEM((rows, 128), f32) for rows in (584, 296, 152, 88)
]


def wave_kernel(
    own, r1, r2, r3, nxt, prv, state_in, state, model, ext, l0, l1, l2, l3, *bufs
):
    wave_update(own, r1, r2, r3, nxt, prv, state_in, state, ext, (l0, l1, l2, l3))
    synth_from(state, bufs, model)


def last_kernel(own, r1, r2, r3, nxt, prv, state_in, out, state, ext, l0, l1, l2, l3):
    wave_update(own, r1, r2, r3, nxt, prv, state_in, state, ext, (l0, l1, l2, l3))
    for g in range(6):
        n = SEG_ROWS[g]
        base = SEG_OFF[g]
        tile = state[base + 8 : base + 8 + n, :].T
        for q in range(4):
            out[:, COEF_OFF[g] + q * n : COEF_OFF[g] + (q + 1) * n] = tile[32 * q : 32 * q + 32, :]


def from_ahead(x, axis, by):
    n = lax.axis_size(axis)
    return lax.ppermute(x, axis, [(i, (i - by) % n) for i in range(n)])


def to_ahead(x, axis, by):
    n = lax.axis_size(axis)
    return lax.ppermute(x, axis, [(i, (i + by) % n) for i in range(n)])


def by_core(x, stage, by):
    pairs = []
    for i in range(4):
        for j in range(4):
            for c in range(2):
                to = (i, (j + by) % 4) if c == stage else ((i + by) % 4, j)
                pairs.append((8 * i + 2 * j + c, 8 * to[0] + 2 * to[1] + c))
    return lax.ppermute(x, MP, pairs)


MP = ("x", "z", "core")


def three(xs, move):
    out = []
    for k in (1, 2, 3):
        out.append(move(xs[k - 1], k))
    return out


def along(x, by):
    return lax.ppermute(x, MP, [(i, (i + by) % 32) for i in range(32)])


def body(coeffs_start, observed, jacobian_tiles, tile_rows, tile_cols, tile_count):
    jac = jacobian_tiles[0, 0]
    rows = tile_rows[0, 0]
    cols = tile_cols[0, 0]
    cnt = tile_count[0]
    n_slots = jac.shape[0]
    table = jnp.concatenate([rows, cols, cnt])
    x, z, core = (lax.axis_index(a) for a in ("x", "z", "core"))
    tiles = sds((8, 128, 128), f32)
    tiles_b = sds((8, 128, 128), bf16)
    flat_b = sds((1024, 128), bf16)

    state, tails = call(
        init_kernel, [VM], [sds((STATE_ROWS, 128), f32), sds((48, 128), f32)]
    )(coeffs_start.T)
    obs_all = observed.reshape(4, 4, 2, 256, 128)
    obs_rows = lax.cond(
        core == 0,
        lambda a: lax.dynamic_slice(a, (0, z, 0, 0, 0), (4, 1, 1, 256, 128)).reshape(4, 256, 128),
        lambda a: lax.dynamic_slice(a, (x, 0, 1, 0, 0), (1, 4, 1, 256, 128)).reshape(4, 256, 128),
        obs_all,
    )
    (obs_t,) = call(obs_kernel, [VM], [tiles])(obs_rows)
    recv = along(tails, 1)
    (model,) = call(early_kernel, [VM], [flat_b], SYNTH_BUFS)(state)
    state, fix = call(
        synth_kernel,
        [VM, VM],
        [sds((STATE_ROWS, 128), f32), sds((128, 128), bf16)],
        SYNTH_BUFS + [pltpu.VMEM((1024, 128), bf16)],
    )(state, recv)

    jac_scratch = pltpu.VMEM((n_slots, TILE, TILE), bf16)
    sems = pltpu.SemaphoreType.DMA((n_slots // CHUNK,))
    for sweep in range(ITERS):
        pull = lambda a, k: from_ahead(a, "ray", k)
        push = lambda a, k: to_ahead(a, "ray", k)
        pieces = [model] + three([model] * 3, pull)
        fixes = []
        if sweep == 0:
            fixes = [fix] + three([fix] * 3, pull)
        keep, send = call(
            fwd_kernel if sweep else first_kernel,
            [SM] + [VM] * (4 + len(fixes)) + [ANY],
            [sds((32, 128, 128), f32), sds((32, 128, 128), bf16)],
            [jac_scratch, pltpu.VMEM((32, 128, 128), bf16), pltpu.VMEM((65, 128, 128), f32), sems],
        )(table, *fixes, *pieces, jac)
        got = to_ahead(send, "core", 1)
        own, s1, s2, s3 = call(
            split_kernel, [VM, VM], [tiles, tiles_b, tiles_b, tiles_b]
        )(keep, got)
        r = three((s1, s2, s3), lambda a, k: by_core(a, 0, k))
        own, sent = call(gather_kernel, [VM] * 4, [tiles, tiles_b])(own, *r)
        r = three([sent] * 3, lambda a, k: by_core(a, 1, k))
        (rounded,) = call(misfit_kernel, [VM] * 5, [tiles_b])(own, *r, obs_t)
        if sweep == ITERS - 1:
            (share,) = call(share_kernel, [VM] * 5, [sds((256, 128), f32)])(
                own, *r, obs_t
            )
        mine = [rounded] + three([rounded] * 3, lambda a, k: by_core(a, 0, -k))
        other = [to_ahead(m, "core", 1) for m in mine]
        edge, edge_b = sds((32, 128), f32), sds((32, 128), bf16)
        g0, g1, g2, g3, e0, e1, e2, e3 = call(
            bwd_kernel,
            [SM] + [VM] * 8 + [ANY],
            [tiles, tiles_b, tiles_b, tiles_b, edge, edge_b, edge_b, edge_b],
            [jac_scratch, pltpu.VMEM((64, 128, 128), bf16), pltpu.VMEM((33, 128, 128), f32), sems],
        )(table, *mine, *other, jac)
        r = three((e1, e2, e3), push)
        (near,) = call(edge_kernel, [VM] * 4, [edge])(e0, *r)
        nxt = along(near, -1)
        prv = along(near, 1) if sweep < ITERS - 1 else near
        r = three((g1, g2, g3), push)
        if sweep < ITERS - 1:
            state, model = call(
                wave_kernel, [VM] * 7, [sds((STATE_ROWS, 128), f32), flat_b], WAVE_BUFS + SYNTH_BUFS
            )(g0, *r, nxt, prv, state)
        else:
            (coeffs,) = call(
                last_kernel,
                [VM] * 7,
                [sds((32, 4096), f32)],
                [pltpu.VMEM((STATE_ROWS, 128), f32)] + WAVE_BUFS,
            )(g0, *r, nxt, prv, state)
    return (coeffs.T, share)


def solution(mesh):
    fine = Mesh(mesh.devices.reshape(4, 4, 4, 2), ("ray", "x", "z", "core"))
    placed = (
        P(MP, "ray"),
        P("ray", None),
        P("ray", MP, None, None, None),
        P("ray", MP, None),
        P("ray", MP, None),
        P("ray", MP),
    )
    return jax.shard_map(
        body,
        mesh=fine,
        in_specs=placed,
        out_specs=(P(MP, "ray"), P(("ray",) + MP, None)),
        check_vma=False,
    )
```

```python
import math

import jax
import jax.numpy as jnp
from jax import lax
from jax.experimental import pallas as pl
from jax.experimental.pallas import tpu as pltpu
from jax.sharding import Mesh, PartitionSpec as P


LEVELS = 5
ITERS = 2
TILE = 128
FWD_GROUP = 48
BWD_GROUP = 64
CHUNK = 16
ROW_BLOCKS = 64
CELL_TILES = 32


root_three = math.sqrt(3.0)
norm_factor = 4.0 * math.sqrt(2.0)
low_pass = [
    (1.0 + root_three) / norm_factor,
    (3.0 + root_three) / norm_factor,
    (3.0 - root_three) / norm_factor,
    (1.0 - root_three) / norm_factor,
]
high_pass = [low_pass[3], -low_pass[2], low_pass[1], -low_pass[0]]
step_length = 0.5
threshold = 0.1

f32 = jnp.float32
bf16 = jnp.bfloat16

SEG_ROWS = [512, 256, 128, 64, 32, 32]
SEG_OFF = [0]
for n in SEG_ROWS:
    SEG_OFF.append(SEG_OFF[-1] + 8 + n)
STATE_ROWS = SEG_OFF[-1]
COEF_OFF = [0, 2048, 3072, 3584, 3840, 3968]

VM = pl.BlockSpec(memory_space=pltpu.VMEM)
SM = pl.BlockSpec(memory_space=pltpu.SMEM)
ANY = pl.BlockSpec(memory_space=pl.ANY)


def sds(shape, dtype):
    return jax.ShapeDtypeStruct(shape, dtype)


def call(kernel, in_specs, outs, scratch=(), mib=40):
    return pl.pallas_call(
        kernel,
        in_specs=in_specs,
        out_specs=[VM] * len(outs),
        out_shape=outs,
        scratch_shapes=list(scratch),
        compiler_params=pltpu.CompilerParams(vmem_limit_bytes=mib * 1024 * 1024),
    )


def lanes(shape):
    return lax.broadcasted_iota(jnp.int32, shape, 1)


def init_kernel(coeffs, state, tails):
    for g in range(6):
        n = SEG_ROWS[g]
        base = SEG_OFF[g]
        parts = [coeffs[:, COEF_OFF[g] + q * n : COEF_OFF[g] + (q + 1) * n] for q in range(4)]
        packed = jnp.concatenate(parts, axis=0).T
        state[base + 8 : base + 8 + n, :] = packed
        last = packed[n - 8 : n, :]
        state[base : base + 8, :] = pltpu.roll(last, 32, 1)
        tails[8 * g : 8 * g + 8, :] = last


def axes(core):
    x, z = lax.axis_index("x"), lax.axis_index("z")
    first = jnp.where(core == 0, z, x)
    second = jnp.where(core == 0, x, z)
    step = jnp.where(core == 0, 1, 4)
    return first, second, step, 5 - step


def tile_copies(jac, jbuf, sems, live, size):
    def copy(i):
        part = pl.ds(i * CHUNK, CHUNK)
        return pltpu.make_async_copy(jac.at[part], jbuf.at[part], sems.at[i])

    groups = (live + size - 1) // size
    per = size // CHUNK

    for i in range(jac.shape[0] // CHUNK):
        @pl.when(i < groups * per)
        def _():
            copy(i).start()

    def arrive(g):
        for i in range(per):
            copy(g * per + i).wait()

    return groups, arrive


def synth_from(state, bufs, model):
    src = None
    for level in reversed(range(LEVELS)):
        n = SEG_ROWS[level]
        base = SEG_OFF[level]
        if src is None:
            sm = state[SEG_OFF[5] + 4 : SEG_OFF[5] + 8 + n, :]
            sp = state[SEG_OFF[5] + 3 : SEG_OFF[5] + 7 + n, :]
        else:
            sm = src[4 : 8 + n, :]
            sp = src[3 : 7 + n, :]
        dm = state[base + 4 : base + 8 + n, :]
        dp = state[base + 3 : base + 7 + n, :]
        even = low_pass[0] * sm + high_pass[0] * dm + low_pass[2] * sp + high_pass[2] * dp
        odd = low_pass[1] * sm + high_pass[1] * dm + low_pass[3] * sp + high_pass[3] * dp
        dst = bufs[level]
        dst[pl.ds(0, n + 4, stride=2), :] = even
        dst[pl.ds(1, n + 4, stride=2), :] = odd
        src = dst
    model[...] = src[8:1032, :].astype(bf16)


SYNTH_BUFS = [pltpu.VMEM((8 + 2 * SEG_ROWS[l], 128), f32) for l in range(LEVELS)]


def early_kernel(state, model, *bufs):
    synth_from(state, bufs, model)


def synth_kernel(state_in, recv, state, fix, *scratch):
    state[...] = state_in[...]
    for g in range(6):
        base = SEG_OFF[g]
        own = state_in[base : base + 8, :]
        got = pltpu.roll(recv[8 * g : 8 * g + 8, :], 32, 1)
        state[base : base + 8, :] = jnp.where(lanes((8, 128)) < 32, got, own)
    model = scratch[-1]
    synth_from(state, scratch[:-1], model)
    fix[...] = model[0:128, :]


def first_kernel(rows, cols, cnt, f0, f1, f2, f3, *refs):
    fwd_kernel(rows, cols, cnt, *refs, fixes=(f0, f1, f2, f3))


def fwd_kernel(
    rows, cols, cnt, p0, p1, p2, p3, jac, keep, send, jbuf, model, acc, sems, fixes=None
):
    live = cnt[0]
    core = lax.axis_index("core")
    groups, arrive = tile_copies(jac, jbuf, sems, live, FWD_GROUP)
    acc[...] = jnp.zeros(acc.shape, f32)
    for c in range(CELL_TILES):
        q, t = c // 8, c % 8
        pieces = fixes if c == 0 and fixes else (p0, p1, p2, p3)
        model[c] = jnp.concatenate(
            [p[128 * t : 128 * t + 128, 32 * q : 32 * q + 32] for p in pieces], axis=1
        )

    def group(g, carry):
        arrive(g)
        for v in range(FWD_GROUP):
            s = g * FWD_GROUP + v
            r = jnp.where(s < live, rows[s], ROW_BLOCKS)
            acc[r] += jnp.dot(jbuf[s], model[cols[s]], preferred_element_type=f32)
        return carry

    lax.fori_loop(0, groups, group, 0)
    for xz in range(16):
        for h in range(2):
            keep[2 * xz + h] = acc[4 * xz + 2 * core + h]
            send[2 * xz + h] = acc[4 * xz + 2 * (1 - core) + h].astype(bf16)


def split_kernel(keep, recv, own, s1, s2, s3):
    first, _, step, other = axes(lax.axis_index("core"))
    for k, out in enumerate((own, s1, s2, s3)):
        for e in range(4):
            for h in range(2):
                b = 2 * (step * ((first + k) % 4) + other * e) + h
                out[2 * e + h] = (keep[b] + recv[b].astype(f32)).astype(out.dtype)


def gather_kernel(own, r1, r2, r3, total, sent):
    for i in range(8):
        s = own[i] + r1[i].astype(f32) + r2[i].astype(f32) + r3[i].astype(f32)
        total[i] = s
        sent[i] = s.astype(bf16)


def misfit_tile(own, r1, r2, r3, obs, i):
    return own[i] + r1[i].astype(f32) + r2[i].astype(f32) + r3[i].astype(f32) - obs[i]


def obs_kernel(obs, out):
    back = (128 - 32 * lax.axis_index("ray")) % 128
    for i in range(8):
        out[i] = pltpu.roll(obs[i // 2, 128 * (i % 2) : 128 * (i % 2) + 128, :], back, 1)


def misfit_kernel(own, r1, r2, r3, obs, rounded):
    for i in range(8):
        rounded[i] = misfit_tile(own, r1, r2, r3, obs, i).T.astype(bf16)


def share_kernel(own, r1, r2, r3, obs, share):
    for h in range(2):
        tile = misfit_tile(own, r1, r2, r3, obs, 2 * axes(lax.axis_index("core"))[1] + h)
        share[128 * h : 128 * h + 128, :] = pltpu.roll(tile, 32 * lax.axis_index("ray"), 1)


def bwd_kernel(table, *refs):
    jac, g0, g1, g2, g3, edge, jbuf, mis, acc, sems = refs[8:]
    slots = jac.shape[0]
    live = table[2 * slots]
    core = lax.axis_index("core")
    groups, arrive = tile_copies(jac, jbuf, sems, live, BWD_GROUP)
    acc[...] = jnp.zeros(acc.shape, f32)
    for pieces, c in ((refs[0:4], core), (refs[4:8], 1 - core)):
        first, _, step, other = axes(c)
        for k in range(4):
            b = 4 * step * ((first + k) % 4) + 2 * c
            for e in range(4):
                for h in range(2):
                    mis[b + 4 * other * e + h] = pieces[k][2 * e + h]

    def group(g, carry):
        arrive(g)
        for v in range(BWD_GROUP):
            s = g * BWD_GROUP + v
            c = jnp.where(s < live, table[slots + s], CELL_TILES)
            acc[c] += jnp.dot(mis[table[s]], jbuf[s], preferred_element_type=f32)
        return carry

    lax.fori_loop(0, groups, group, 0)
    edge[...] = jnp.where(lanes((128, 128)) < 64, acc[0], acc[CELL_TILES - 1]).astype(bf16)
    for k, out in enumerate((g0, g1, g2, g3)):
        for t in range(8):
            for q in range(4):
                out[t, 32 * q : 32 * q + 32, :] = acc[8 * q + t, 32 * k : 32 * k + 32, :].astype(out.dtype)


def edge_kernel(nxt, prv, *out):
    both = jnp.where(lanes((128, 128)) < 64, nxt[...], prv[...])
    for k in range(4):
        out[k][...] = both[32 * k : 32 * k + 32, :]


def wave_update(own, r1, r2, r3, e0, e1, e2, e3, state_in, state, ext, levels):
    for i in range(8):
        s = own[i] + r1[i].astype(f32) + r2[i].astype(f32) + r3[i].astype(f32)
        ext[64 + 128 * i : 192 + 128 * i, :] = s.T
    ln = lanes((64, 128))
    edge = e0[...].astype(f32)
    for e in (e1, e2, e3):
        edge += e[...].astype(f32)
    near = jnp.concatenate([edge, jnp.zeros((64, 128), f32), edge], axis=0).T
    ext[0:64, :] = jnp.where(ln < 32, near[64:, :], pltpu.roll(ext[1024:1088, :], 32, 1))
    ext[1088:1152, :] = jnp.where(ln >= 96, near[:64, :], pltpu.roll(ext[64:128, :], 96, 1))
    ext[1152:1160, :] = jnp.zeros((8, 128), f32)
    src = ext
    for level in range(LEVELS):
        count = [576, 288, 144, 72, 40][level]
        front = 64 >> (level + 1)
        n = SEG_ROWS[level]
        base = SEG_OFF[level]
        e0 = src[pl.ds(0, count, stride=2), :]
        o0 = src[pl.ds(1, count, stride=2), :]
        e1 = src[pl.ds(2, count, stride=2), :]
        o1 = src[pl.ds(3, count, stride=2), :]
        smooth = low_pass[0] * e0 + low_pass[1] * o0 + low_pass[2] * e1 + low_pass[3] * o1
        detail = high_pass[0] * e0 + high_pass[1] * o0 + high_pass[2] * e1 + high_pass[3] * o1
        lead = min(front, 8)
        part = detail[front - lead : front + n, :]
        moved = state_in[base + 8 - lead : base + 8 + n, :] - step_length * part
        state[base + 8 - lead : base + 8 + n, :] = moved - jnp.clip(moved, -threshold, threshold)
        if lead < 8:
            state[base : base + 8 - lead, :] = jnp.zeros((8 - lead, 128), f32)
        if level < LEVELS - 1:
            dst = levels[level]
            dst[0:count, :] = smooth
            dst[count:, :] = jnp.zeros((dst.shape[0] - count, 128), f32)
            src = dst
        else:
            base = SEG_OFF[5]
            part = smooth[front - lead : front + n, :]
            state[base + 8 - lead : base + 8 + n, :] = (
                state_in[base + 8 - lead : base + 8 + n, :] - step_length * part
            )
            state[base : base + 8 - lead, :] = jnp.zeros((8 - lead, 128), f32)


WAVE_BUFS = [pltpu.VMEM((1160, 128), f32)] + [
    pltpu.VMEM((rows, 128), f32) for rows in (584, 296, 152, 88)
]


def wave_kernel(
    own, r1, r2, r3, e0, e1, e2, e3, state_in, state, model, ext, l0, l1, l2, l3, *bufs
):
    wave_update(own, r1, r2, r3, e0, e1, e2, e3, state_in, state, ext, (l0, l1, l2, l3))
    synth_from(state, bufs, model)


def last_kernel(
    own, r1, r2, r3, e0, e1, e2, e3, state_in, out, state, ext, l0, l1, l2, l3
):
    wave_update(own, r1, r2, r3, e0, e1, e2, e3, state_in, state, ext, (l0, l1, l2, l3))
    for g in range(6):
        n = SEG_ROWS[g]
        base = SEG_OFF[g]
        tile = state[base + 8 : base + 8 + n, :].T
        for q in range(4):
            out[:, COEF_OFF[g] + q * n : COEF_OFF[g] + (q + 1) * n] = tile[32 * q : 32 * q + 32, :]


def from_ahead(x, axis, by):
    n = lax.axis_size(axis)
    return lax.ppermute(x, axis, [(i, (i - by) % n) for i in range(n)])


def to_ahead(x, axis, by):
    n = lax.axis_size(axis)
    return lax.ppermute(x, axis, [(i, (i + by) % n) for i in range(n)])


def by_core(x, stage, by):
    pairs = []
    for i in range(4):
        for j in range(4):
            for c in range(2):
                to = (i, (j + by) % 4) if c == stage else ((i + by) % 4, j)
                pairs.append((8 * i + 2 * j + c, 8 * to[0] + 2 * to[1] + c))
    return lax.ppermute(x, MP, pairs)


MP = ("x", "z", "core")


def three(xs, move):
    out = []
    for k in (1, 2, 3):
        out.append(move(xs[k - 1], k))
    return out


def along(x, by):
    return lax.ppermute(x, MP, [(i, (i + by) % 32) for i in range(32)])


def body(coeffs_start, observed, jacobian_tiles, tile_rows, tile_cols, tile_count):
    jac = jacobian_tiles[0, 0]
    rows = tile_rows[0, 0]
    cols = tile_cols[0, 0]
    cnt = tile_count[0]
    n_slots = jac.shape[0]
    table = jnp.concatenate([rows, cols, cnt])
    x, z, core = (lax.axis_index(a) for a in ("x", "z", "core"))
    tiles = sds((8, 128, 128), f32)
    tiles_b = sds((8, 128, 128), bf16)
    flat_b = sds((1024, 128), bf16)

    state, tails = call(
        init_kernel, [VM], [sds((STATE_ROWS, 128), f32), sds((48, 128), f32)]
    )(coeffs_start.T)
    obs_all = observed.reshape(4, 4, 2, 256, 128)
    obs_rows = lax.cond(
        core == 0,
        lambda a: lax.dynamic_slice(a, (0, z, 0, 0, 0), (4, 1, 1, 256, 128)).reshape(4, 256, 128),
        lambda a: lax.dynamic_slice(a, (x, 0, 1, 0, 0), (1, 4, 1, 256, 128)).reshape(4, 256, 128),
        obs_all,
    )
    (obs_t,) = call(obs_kernel, [VM], [tiles])(obs_rows)
    recv = along(tails, 1)
    (model,) = call(early_kernel, [VM], [flat_b], SYNTH_BUFS)(state)
    state, fix = call(
        synth_kernel,
        [VM, VM],
        [sds((STATE_ROWS, 128), f32), sds((128, 128), bf16)],
        SYNTH_BUFS + [pltpu.VMEM((1024, 128), bf16)],
    )(state, recv)

    jac_scratch = pltpu.VMEM((n_slots, TILE, TILE), bf16)
    sems = pltpu.SemaphoreType.DMA((n_slots // CHUNK,))
    for sweep in range(ITERS):
        pull = lambda a, k: from_ahead(a, "ray", k)
        push = lambda a, k: to_ahead(a, "ray", k)
        pieces = [model] + three([model] * 3, pull)
        fixes = []
        if sweep == 0:
            fixes = [fix] + three([fix] * 3, pull)
        keep, send = call(
            fwd_kernel if sweep else first_kernel,
            [SM] * 3 + [VM] * (4 + len(fixes)) + [ANY],
            [sds((32, 128, 128), f32), sds((32, 128, 128), bf16)],
            [jac_scratch, pltpu.VMEM((32, 128, 128), bf16), pltpu.VMEM((65, 128, 128), f32), sems],
        )(rows, cols, cnt, *fixes, *pieces, jac)
        got = to_ahead(send, "core", 1)
        own, s1, s2, s3 = call(
            split_kernel, [VM, VM], [tiles, tiles_b, tiles_b, tiles_b]
        )(keep, got)
        r = three((s1, s2, s3), lambda a, k: by_core(a, 0, k))
        own, sent = call(gather_kernel, [VM] * 4, [tiles, tiles_b])(own, *r)
        r = three([sent] * 3, lambda a, k: by_core(a, 1, k))
        (rounded,) = call(misfit_kernel, [VM] * 5, [tiles_b])(own, *r, obs_t)
        if sweep == ITERS - 1:
            (share,) = call(share_kernel, [VM] * 5, [sds((256, 128), f32)])(
                own, *r, obs_t
            )
        mine = [rounded] + three([rounded] * 3, lambda a, k: by_core(a, 0, -k))
        other = [to_ahead(m, "core", 1) for m in mine]
        g0, g1, g2, g3, edge = call(
            bwd_kernel,
            [SM] + [VM] * 8 + [ANY],
            [tiles, tiles_b, tiles_b, tiles_b, sds((128, 128), bf16)],
            [jac_scratch, pltpu.VMEM((64, 128, 128), bf16), pltpu.VMEM((33, 128, 128), f32), sems],
        )(table, *mine, *other, jac)
        r = three((g1, g2, g3), push)
        nxt = along(edge, -1)
        prv = along(edge, 1) if sweep < ITERS - 1 else edge
        e0, *es = call(edge_kernel, [VM] * 2, [sds((32, 128), bf16)] * 4)(nxt, prv)
        es = [e0] + three(es, push)
        if sweep < ITERS - 1:
            state, model = call(
                wave_kernel, [VM] * 9, [sds((STATE_ROWS, 128), f32), flat_b], WAVE_BUFS + SYNTH_BUFS
            )(g0, *r, *es, state)
        else:
            (coeffs,) = call(
                last_kernel,
                [VM] * 9,
                [sds((32, 4096), f32)],
                [pltpu.VMEM((STATE_ROWS, 128), f32)] + WAVE_BUFS,
            )(g0, *r, *es, state)
    return (coeffs.T, share)


def solution(mesh):
    fine = Mesh(mesh.devices.reshape(4, 4, 4, 2), ("ray", "x", "z", "core"))
    placed = (
        P(MP, "ray"),
        P("ray", None),
        P("ray", MP, None, None, None),
        P("ray", MP, None),
        P("ray", MP, None),
        P("ray", MP),
    )
    return jax.shard_map(
        body,
        mesh=fine,
        in_specs=placed,
        out_specs=(P(MP, "ray"), P(("ray",) + MP, None)),
        check_vma=False,
    )
```
